256 devices in a mesh: img: 16 (over y, z_hi, core), depth: 16 (over x, z_lo).
Axes of the slice: x: 4, y: 4, z: 8 (z_hi: 2, z_lo: 4; z = z_hi * 4 + z_lo), core: 2. Of those that a mesh axis runs over, the one named last changes fastest.
Arguments:
- counts: int32 [512, 1024, 512], P('depth', 'img'), may hold values from 0 to 5, as said below
Outputs:
- image: float32 [4, 1024, 512], P(None, ('img', 'depth'))
The draws below stay inside these ranges and needn't reach their ends.
Inputs may be any that keep to these rules, and one draw needn't show every extreme that they name: `counts`: whole numbers of atoms.
All inputs are finite; a program needn't handle non-finite values.
Results may differ from the reference program's by a relative error of at most 0.0003.
Values sent between devices are 32-bit elements; how exact they have to be, the bound alone decides.
A program may use at most 64 MiB of HBM per device.

```python
import math
import jax
import jax.numpy as jnp
from jax import lax

CX = 64
NX = 1024
NY = 512
NZ = 512


def piecewise_counts(seed_key, depth_cell, row_cell, column_cell, levels):
    coarse = jax.random.randint(seed_key, (NZ // depth_cell + 2, NX // row_cell + 2, NY // column_cell + 2), 0, levels, dtype=jnp.int32)
    spread_out = jnp.repeat(jnp.repeat(jnp.repeat(coarse, depth_cell, 0), row_cell, 1), column_cell, 2)
    start_key = jax.random.fold_in(seed_key, 7)
    depth_start = jax.random.randint(jax.random.fold_in(start_key, 1), (), 0, depth_cell, dtype=jnp.int32)
    row_start = jax.random.randint(jax.random.fold_in(start_key, 2), (), 0, row_cell, dtype=jnp.int32)
    column_start = jax.random.randint(jax.random.fold_in(start_key, 3), (), 0, column_cell, dtype=jnp.int32)
    return lax.dynamic_slice(spread_out, (depth_start, row_start, column_start), (NZ, NX, NY))


def draw_counts(key, part):
    broad_part = piecewise_counts(jax.random.fold_in(key, 11), 32, 32, 32, 2)
    layer_part = piecewise_counts(jax.random.fold_in(key, 12), 1, 8, 8, 4)
    row_part = piecewise_counts(jax.random.fold_in(key, 14), 32, 1, 8, 3)
    jitter = jax.random.randint(jax.random.fold_in(key, 13), (NZ, NX, NY), 0, 2, dtype=jnp.int32)
    values = jnp.clip(broad_part + layer_part + row_part + jitter - 1, 0, 5)
    values = values.at[0, 0, 0].set(0)
    values = values.at[NZ - 1, NX - 1, NY - 1].set(5)
    return values.astype(jnp.int32)


def setup_inputs(seed: int = 0) -> dict:
    key_of = jax.random.split(jax.random.key(seed), 2)
    return {
        "counts": draw_counts(jax.random.fold_in(key_of[1], 71), 0),
    }


gauss_taps = [math.exp(-offset * offset / 8.0) / sum(math.exp(-other * other / 8.0) for other in range(-4, 5)) for offset in range(-4, 5)]
light_z = 0.48
light_x = 0.6
light_y = 0.64


def smooth_valid(values, axis):
    length = values.shape[axis] - 8
    total = gauss_taps[0] * lax.slice_in_dim(values, 0, length, axis=axis)
    for offset in range(1, 9):
        total = total + gauss_taps[offset] * lax.slice_in_dim(values, offset, offset + length, axis=axis)
    return total


def smooth_last(values):
    widths = [(0, 0)] * (values.ndim - 1) + [(4, 4)]
    return smooth_valid(jnp.pad(values, widths), values.ndim - 1)


def render_terms(smooth_ext, depth_total):
    smoothed = smooth_ext[1:-1, 1:-1, :]
    grad_z = 0.5 * (smooth_ext[2:, 1:-1, :] - smooth_ext[:-2, 1:-1, :])
    grad_x = 0.5 * (smooth_ext[1:-1, 2:, :] - smooth_ext[1:-1, :-2, :])
    padded = jnp.pad(smoothed, ((0, 0), (0, 0), (1, 1)))
    grad_y = 0.5 * (padded[:, :, 2:] - padded[:, :, :-2])
    shading = 0.55 + 0.45 * jnp.tanh(3.0 * (light_z * grad_z + light_x * grad_x + light_y * grad_y))
    gradient_sq = grad_z * grad_z + grad_x * grad_x + grad_y * grad_y
    optical = (1.5 / depth_total) * smoothed * smoothed / (1.0 + smoothed * smoothed) * (1.0 + 4.0 * gradient_sq)
    sigma_red = jax.nn.sigmoid(2.0 * (smoothed - 2.5))
    red_light = shading * sigma_red
    green_light = shading * jnp.exp(-(smoothed - 2.5) ** 2)
    blue_light = shading * (1.0 - sigma_red)
    return optical, red_light, green_light, blue_light


def integrate(optical, red_light, green_light, blue_light):
    before = jnp.cumsum(optical, axis=0) - optical
    weight = jnp.exp(-before) * (1.0 - jnp.exp(-optical))
    colors = jnp.stack([jnp.sum(weight * red_light, 0), jnp.sum(weight * green_light, 0), jnp.sum(weight * blue_light, 0)], 0)
    transmit = jnp.exp(-jnp.sum(optical, 0))
    return colors, transmit


def reference(counts):
    density = counts.astype(jnp.float32)
    depth_total, rows_total, columns = density.shape
    padded = jnp.pad(density, ((0, 0), (5, 5), (0, 0)))

    def one_block(block_number):
        offset = (block_number * CX).astype(jnp.int32)
        window_field = lax.dynamic_slice_in_dim(padded, offset, CX + 10, 1)
        window_field = smooth_last(window_field)
        window_field = smooth_valid(window_field, 1)
        window_field = smooth_valid(jnp.pad(window_field, ((4, 4), (0, 0), (0, 0))), 0)
        x_cells = offset - 1 + jnp.arange(CX + 2, dtype=jnp.int32)
        inside = (x_cells >= 0) & (x_cells < rows_total)
        window_field = jnp.where(inside[None, :, None], window_field, jnp.zeros_like(window_field))
        smooth_ext = jnp.pad(window_field, ((1, 1), (0, 0), (0, 0)))
        colors, transmit = integrate(*render_terms(smooth_ext, depth_total))
        return jnp.concatenate([colors, (1.0 - transmit)[None]], 0)

    blocks = lax.map(one_block, jnp.arange(rows_total // CX, dtype=jnp.int32))
    return jnp.transpose(blocks, (1, 0, 2, 3)).reshape(4, rows_total, columns)
```

```python
import math

import jax
import jax.numpy as jnp
import numpy as np
from jax import lax
from jax.experimental import pallas as pl
from jax.experimental.pallas import tpu as pltpu
from jax.sharding import PartitionSpec as P
import ml_dtypes

gauss_taps = [
    math.exp(-offset * offset / 8.0)
    / sum((math.exp(-other * other / 8.0) for other in range(-4, 5)))
    for offset in range(-4, 5)
]
MESH = pl.DeviceIdType.MESH
f32 = jnp.float32
bf16 = jnp.bfloat16


def split_taps(matrix):
    high = matrix.astype(np.float32).astype(ml_dtypes.bfloat16).astype(np.float64)
    low = (matrix - high).astype(np.float32).astype(ml_dtypes.bfloat16).astype(np.float64)
    return high, low


def column_matrix(columns):
    index = np.arange(columns)
    offset = index[:, None] - index[None, :]
    matrix = np.zeros((columns, columns))
    for k in range(-4, 5):
        matrix[offset == k] = gauss_taps[k + 4]
    high, low = split_taps(matrix)
    return np.stack([high, low]).astype(ml_dtypes.bfloat16)


def row_matrix(rows):
    target = np.full((rows + 16,), 10**6)
    target[7 : rows + 9] = np.arange(-1, rows + 1)
    source = np.full((rows + 16,), -(10**6))
    source[:rows] = np.arange(rows)
    source[rows : rows + 5] = np.arange(-5, 0)
    source[rows + 8 : rows + 13] = np.arange(rows, rows + 5)
    offset = source[None, :] - target[:, None]
    matrix = np.zeros(offset.shape)
    for k in range(-4, 5):
        matrix[offset == k] = gauss_taps[k + 4]
    high, low = split_taps(matrix)
    pad = np.zeros((rows + 16, 16))
    return np.concatenate([high, low, high, pad], axis=1).astype(np.float32)


def render_kernel(
    depth_total, img_count, depth_count,
    counts_ref, colmat_ref, rowmat_ref, out_ref,
    cnt, wcol, brow_f, brow, stage, halo, hconv, yhigh, ylow, ufield, sfield,
    pack, pack_in, partial, outbox, inbox,
    load_sem, img_send, img_recv, dep_send, dep_recv, all_send, all_recv,
):
    img = lax.axis_index("img")
    dep = lax.axis_index("depth")
    slab, rows, columns = cnt.shape
    tiles = rows // 8
    owned = rows // depth_count
    ext = rows + 16

    barrier = pltpu.get_barrier_semaphore()
    has_prev, has_next = img > 0, img < img_count - 1
    has_front, has_back = dep > 0, dep < depth_count - 1

    def greet_depth(step, carry):
        target = lax.rem(dep + step, depth_count)
        pl.semaphore_signal(barrier, inc=1, device_id=(img, target), device_id_type=MESH)
        return carry

    lax.fori_loop(1, depth_count, greet_depth, 0)
    for step in (1, img_count - 1):
        pl.semaphore_signal(
            barrier, inc=1, device_id=(lax.rem(img + step, img_count), dep), device_id_type=MESH
        )

    loads = [
        pltpu.make_async_copy(counts_ref, cnt, load_sem.at[0]),
        pltpu.make_async_copy(colmat_ref, wcol, load_sem.at[1]),
        pltpu.make_async_copy(rowmat_ref, brow_f, load_sem.at[2]),
    ]
    for load in loads:
        load.start()

    ylow[:, ext:, :] = jnp.zeros((slab, 16, columns), bf16)
    hconv[...] = jnp.zeros(hconv.shape, f32)

    @pl.when(jnp.logical_not(has_prev))
    def _():
        halo[0] = jnp.zeros(halo.shape[1:], jnp.int32)

    @pl.when(jnp.logical_not(has_next))
    def _():
        halo[1] = jnp.zeros(halo.shape[1:], jnp.int32)

    @pl.when(jnp.logical_not(has_front))
    def _():
        ufield[0:5] = jnp.zeros((5, ext, columns), f32)
        pack_in[0] = jnp.zeros(pack_in.shape[1:], f32)

    @pl.when(jnp.logical_not(has_back))
    def _():
        ufield[slab + 5 :] = jnp.zeros((5, ext, columns), f32)
        pack_in[1] = jnp.zeros(pack_in.shape[1:], f32)

    for load in loads:
        load.wait()

    for group in range(slab // 8):
        for r in range(5):
            stage[0, group, r] = cnt[group * 8 : group * 8 + 8, r, :]
            stage[1, group, r] = cnt[group * 8 : group * 8 + 8, rows - 5 + r, :]

    row_id = lax.broadcasted_iota(jnp.int32, brow_f.shape, 0)
    outside = ((row_id == 7) & (img == 0)) | ((row_id == rows + 8) & (img == img_count - 1))
    brow[...] = jnp.where(outside, 0.0, brow_f[...]).astype(bf16)

    pl.semaphore_wait(barrier, depth_count + 1)

    def img_copy(side, group):
        target = lax.rem(img + (img_count - 1 if side == 0 else 1), img_count)
        return pltpu.make_async_remote_copy(
            src_ref=stage.at[side, group],
            dst_ref=halo.at[1 - side, group],
            send_sem=img_send.at[side, group],
            recv_sem=img_recv.at[1 - side, group],
            device_id=(target, dep),
            device_id_type=MESH,
        )

    groups = slab // 8
    order = [0, groups - 1] + list(range(1, groups - 1))
    for group in order:
        for side, exists in ((0, has_prev), (1, has_next)):
            @pl.when(exists)
            def _():
                img_copy(side, group).start()

    def column_smooth(block):
        block = block.astype(f32).astype(bf16)
        return jnp.dot(block, wcol[0], preferred_element_type=f32) + jnp.dot(
            block, wcol[1], preferred_element_type=f32
        )

    def halves(value):
        high = value.astype(bf16)
        return high, (value - high.astype(f32)).astype(bf16)

    def own_columns(step, carry):
        at = pl.ds(step * 4, 4)
        smooth = column_smooth(cnt[at].reshape(4 * rows, columns))
        high, low = halves(smooth)
        yhigh[at, :rows, :] = high.reshape(4, rows, columns)
        ylow[at, :rows, :] = low.reshape(4, rows, columns)
        return carry

    lax.fori_loop(0, slab // 4, own_columns, 0)

    def rows_of_group(group):
        for side, exists in ((0, has_prev), (1, has_next)):
            @pl.when(exists)
            def _():
                img_copy(1 - side, group).wait_recv()

        for side in range(2):
            smooth = column_smooth(halo[side, group].reshape(40, columns))
            for r in range(5):
                hconv[:, side * 8 + r, :] = smooth[r * 8 : r * 8 + 8]

        def one_layer(j, carry):
            layer = group * 8 + j
            high, low = halves(hconv[j])
            yhigh[layer, rows:ext, :] = high
            ylow[layer, rows:ext, :] = low
            tall = yhigh[layer]
            field = jnp.concatenate([tall, tall, ylow[layer]], axis=0)
            ufield[layer + 5] = jnp.dot(brow[...], field, preferred_element_type=f32)
            return carry

        lax.fori_loop(0, 8, one_layer, 0)

    def depth_copies(side):
        target = lax.rem(dep + (depth_count - 1 if side == 0 else 1), depth_count)
        source = 5 if side == 0 else slab
        place = slab + 5 if side == 0 else 0
        big = pltpu.make_async_remote_copy(
            src_ref=ufield.at[source : source + 5, 8 : rows + 8, :],
            dst_ref=ufield.at[place : place + 5, 8 : rows + 8, :],
            send_sem=dep_send.at[side, 0],
            recv_sem=dep_recv.at[1 - side, 0],
            device_id=(img, target),
            device_id_type=MESH,
        )
        small = pltpu.make_async_remote_copy(
            src_ref=pack.at[side],
            dst_ref=pack_in.at[1 - side],
            send_sem=dep_send.at[side, 1],
            recv_sem=dep_recv.at[1 - side, 1],
            device_id=(img, target),
            device_id_type=MESH,
        )
        return big, small

    def send_depth(side, exists):
        first = 5 if side == 0 else slab + 1
        for j in range(4):
            pack[side, j : j + 1] = ufield[first + j, 7:8, :]
            pack[side, 4 + j : 5 + j] = ufield[first + j, rows + 8 : rows + 9, :]

        @pl.when(exists)
        def _():
            for copy in depth_copies(side):
                copy.start()

    rows_of_group(0)
    send_depth(0, has_front)
    rows_of_group(groups - 1)
    send_depth(1, has_back)
    for group in range(1, groups - 1):
        rows_of_group(group)

    def depth_smooth(low, high):
        def one_tile(tile, carry):
            r = pl.ds(pl.multiple_of(lax.div(tile, columns // 128) * 8, 8), 8)
            c = pl.ds(pl.multiple_of(lax.rem(tile, columns // 128) * 128, 128), 128)
            held = [ufield[m, r, c] for m in range(low, low + 8)]
            for m in range(low, high):
                held.append(ufield[m + 8, r, c])
                total = gauss_taps[4] * held[4]
                for k in range(4):
                    total = total + gauss_taps[k] * (held[k] + held[8 - k])
                sfield[m, r, c] = total
                held.pop(0)
            return carry

        lax.fori_loop(0, (ext // 8) * (columns // 128), one_tile, 0)

    column_id = lax.broadcasted_iota(jnp.int32, (8, columns), 1)
    at_left, at_right = column_id == 0, column_id == columns - 1

    def shade_layer(layer, tile, state):
        seen, total, red, green = state
        base = 8 + 8 * tile
        here = sfield[layer + 1, base : base + 8, :]
        dz = sfield[layer + 2, base : base + 8, :] - sfield[layer, base : base + 8, :]
        dx = sfield[layer + 1, base + 1 : base + 9, :] - sfield[layer + 1, base - 1 : base + 7, :]
        left = jnp.where(at_left, 0.0, pltpu.roll(here, 1, 1))
        right = jnp.where(at_right, 0.0, pltpu.roll(here, columns - 1, 1))
        dy = right - left
        shading = 0.55 + 0.45 * jnp.tanh(0.72 * dz + 0.9 * dx + 0.96 * dy)
        square = here * here
        bend = dz * dz + dx * dx + dy * dy
        tau = (square * pl.reciprocal(1.0 + square)) * ((1.0 + bend) * (1.5 / depth_total))
        weight = seen * (1.0 - jnp.exp(-tau))
        light = weight * shading
        centred = here - 2.5
        return (
            seen - weight,
            total + light,
            red + light * jnp.tanh(centred),
            green + light * jnp.exp(-(centred * centred)),
        )

    depth_smooth(5, slab - 3)
    zeros = jnp.zeros((8, columns), f32)
    ones = jnp.ones((8, columns), f32)
    for tile in range(tiles):
        state = lax.fori_loop(
            5,
            slab - 5,
            lambda layer, state: shade_layer(layer, tile, state),
            (ones, zeros, zeros, zeros),
        )
        for part in range(4):
            partial[part, tile] = state[part]

    for side, exists in ((1, has_back), (0, has_front)):
        @pl.when(exists)
        def _():
            for copy in depth_copies(1 - side):
                copy.wait_recv()

    for j in range(4):
        ufield[1 + j, 7:8, :] = pack_in[0, j : j + 1]
        ufield[1 + j, rows + 8 : rows + 9, :] = pack_in[0, 4 + j : 5 + j]
        ufield[slab + 5 + j, 7:8, :] = pack_in[1, j : j + 1]
        ufield[slab + 5 + j, rows + 8 : rows + 9, :] = pack_in[1, 4 + j : 5 + j]

    depth_smooth(0, 5)
    depth_smooth(slab - 3, slab + 2)

    @pl.when(jnp.logical_not(has_front))
    def _():
        sfield[0] = jnp.zeros((ext, columns), f32)

    @pl.when(jnp.logical_not(has_back))
    def _():
        sfield[slab + 1] = jnp.zeros((ext, columns), f32)

    def all_copy(target, source):
        return pltpu.make_async_remote_copy(
            src_ref=outbox.at[target],
            dst_ref=inbox.at[source],
            send_sem=all_send.at[target],
            recv_sem=all_recv.at[source],
            device_id=(img, target),
            device_id_type=MESH,
        )

    top_half = lax.broadcasted_iota(jnp.int32, (8, columns), 0) < 4
    for tile in range(tiles):
        state = lax.fori_loop(
            0, 5, lambda layer, state: shade_layer(layer, tile, state), (ones, zeros, zeros, zeros)
        )
        seen = state[0]
        state = (seen * partial[0, tile],) + tuple(
            state[part] + seen * partial[part, tile] for part in range(1, 4)
        )
        seen, total, red, green = lax.fori_loop(
            slab - 5, slab, lambda layer, state: shade_layer(layer, tile, state), state
        )
        outbox[2 * tile, 0:8] = jnp.where(top_half, total, pltpu.roll(red, 4, 0))
        outbox[2 * tile, 8:16] = jnp.where(top_half, green, pltpu.roll(seen, 4, 0))
        outbox[2 * tile + 1, 0:8] = jnp.where(top_half, pltpu.roll(total, 4, 0), red)
        outbox[2 * tile + 1, 8:16] = jnp.where(top_half, pltpu.roll(green, 4, 0), seen)
        for target in (2 * tile, 2 * tile + 1):
            @pl.when(dep != target)
            def _():
                all_copy(target, dep).start()

            @pl.when(dep == target)
            def _():
                inbox[target] = outbox[target]

    def compose(source, state):
        seen, upper, lower = state

        @pl.when(source != dep)
        def _():
            all_copy(source, source).wait_recv()

        first, second = inbox[source, 0:8, :], inbox[source, 8:16, :]
        through = jnp.where(top_half, pltpu.roll(second, 4, 0), second)
        return seen * through, upper + seen * first, lower + seen * second

    seen, upper, lower = lax.fori_loop(0, depth_count, compose, (ones, zeros, zeros))
    total, red = upper[0:4], upper[4:8]
    out_ref[0] = 0.5 * (total + red)
    out_ref[1] = lower[0:4]
    out_ref[2] = 0.5 * (total - red)
    out_ref[3] = 1.0 - seen[0:4]

    for group in range(groups):
        for side, exists in ((0, has_prev), (1, has_next)):
            @pl.when(exists)
            def _():
                img_copy(side, group).wait_send()

    for side, exists in ((0, has_front), (1, has_back)):
        @pl.when(exists)
        def _():
            for copy in depth_copies(side):
                copy.wait_send()

    def finish(target, carry):
        @pl.when(target != dep)
        def _():
            all_copy(target, target).wait_send()

        return carry

    lax.fori_loop(0, depth_count, finish, 0)


def solution(mesh):
    img_count, depth_count = mesh.shape["img"], mesh.shape["depth"]

    def local(counts):
        slab, rows, columns = counts.shape
        ext = rows + 16
        groups = slab // 8

        def body(*refs):
            render_kernel(slab * depth_count, img_count, depth_count, *refs)

        anywhere = pl.BlockSpec(memory_space=pl.ANY)
        return pl.pallas_call(
            body,
            out_shape=jax.ShapeDtypeStruct((4, rows // depth_count, columns), f32),
            in_specs=[anywhere] * 3,
            out_specs=pl.BlockSpec(memory_space=pltpu.VMEM),
            scratch_shapes=[
                pltpu.VMEM((slab, rows, columns), jnp.int32),
                pltpu.VMEM((2, columns, columns), bf16),
                pltpu.VMEM((ext, 3 * ext + 16), f32),
                pltpu.VMEM((ext, 3 * ext + 16), bf16),
                pltpu.VMEM((2, groups, 5, 8, columns), jnp.int32),
                pltpu.VMEM((2, groups, 5, 8, columns), jnp.int32),
                pltpu.VMEM((8, 16, columns), f32),
                pltpu.VMEM((slab, ext, columns), bf16),
                pltpu.VMEM((slab, ext + 16, columns), bf16),
                pltpu.VMEM((slab + 10, ext, columns), f32),
                pltpu.VMEM((slab + 2, ext, columns), f32),
                pltpu.VMEM((2, 8, columns), f32),
                pltpu.VMEM((2, 8, columns), f32),
                pltpu.VMEM((4, rows // 8, 8, columns), f32),
                pltpu.VMEM((depth_count, 16, columns), f32),
                pltpu.VMEM((depth_count, 16, columns), f32),
                pltpu.SemaphoreType.DMA((3,)),
                pltpu.SemaphoreType.DMA((2, groups)),
                pltpu.SemaphoreType.DMA((2, groups)),
                pltpu.SemaphoreType.DMA((2, 2)),
                pltpu.SemaphoreType.DMA((2, 2)),
                pltpu.SemaphoreType.DMA((depth_count,)),
                pltpu.SemaphoreType.DMA((depth_count,)),
            ],
            compiler_params=pltpu.CompilerParams(
                collective_id=0, has_side_effects=True, vmem_limit_bytes=56 << 20
            ),
        )(counts, jnp.asarray(column_matrix(columns)), jnp.asarray(row_matrix(rows)))

    return jax.shard_map(
        local,
        mesh=mesh,
        in_specs=(P("depth", "img", None),),
        out_specs=P(None, ("img", "depth"), None),
        check_vma=False,
    )
```

```python
import math

import jax
import jax.numpy as jnp
import numpy as np
from jax import lax
from jax.experimental import pallas as pl
from jax.experimental.pallas import tpu as pltpu
from jax.sharding import PartitionSpec as P
import ml_dtypes

gauss_taps = [
    math.exp(-offset * offset / 8.0)
    / sum((math.exp(-other * other / 8.0) for other in range(-4, 5)))
    for offset in range(-4, 5)
]
MESH = pl.DeviceIdType.MESH
f32 = jnp.float32
bf16 = jnp.bfloat16


def split_taps(matrix):
    high = matrix.astype(np.float32).astype(ml_dtypes.bfloat16).astype(np.float64)
    low = (matrix - high).astype(np.float32).astype(ml_dtypes.bfloat16).astype(np.float64)
    return high, low


def column_matrix(columns):
    index = np.arange(columns)
    offset = index[:, None] - index[None, :]
    matrix = np.zeros((columns, columns))
    for k in range(-4, 5):
        matrix[offset == k] = gauss_taps[k + 4]
    high, low = split_taps(matrix)
    return np.stack([high, low]).astype(ml_dtypes.bfloat16)


def row_matrix(rows):
    target = np.full((rows + 16,), 10**6)
    target[7 : rows + 9] = np.arange(-1, rows + 1)
    source = np.full((rows + 16,), -(10**6))
    source[:rows] = np.arange(rows)
    source[rows : rows + 5] = np.arange(-5, 0)
    source[rows + 8 : rows + 13] = np.arange(rows, rows + 5)
    offset = source[None, :] - target[:, None]
    matrix = np.zeros(offset.shape)
    for k in range(-4, 5):
        matrix[offset == k] = gauss_taps[k + 4]
    high, low = split_taps(matrix)
    pad = np.zeros((rows + 16, 16))
    return np.concatenate([high, low, high, pad], axis=1).astype(np.float32)


def render_kernel(
    depth_total, img_count, depth_count,
    counts_ref, colmat_ref, rowmat_ref, out_ref,
    cnt, wcol, brow_f, brow, stage, halo, hconv, yhigh, ylow, ufield, sfield,
    pack, pack_in, partial, outbox, inbox,
    load_sem, img_send, img_recv, dep_send, dep_recv, all_send, all_recv,
):
    img = lax.axis_index("img")
    dep = lax.axis_index("depth")
    slab, rows, columns = cnt.shape
    tiles = rows // 8
    owned = rows // depth_count
    ext = rows + 16

    barrier = pltpu.get_barrier_semaphore()
    has_prev, has_next = img > 0, img < img_count - 1
    has_front, has_back = dep > 0, dep < depth_count - 1

    def greet_depth(step, carry):
        target = lax.rem(dep + step, depth_count)
        pl.semaphore_signal(barrier, inc=1, device_id=(img, target), device_id_type=MESH)
        return carry

    lax.fori_loop(1, depth_count, greet_depth, 0)
    for step in (1, img_count - 1):
        pl.semaphore_signal(
            barrier, inc=1, device_id=(lax.rem(img + step, img_count), dep), device_id_type=MESH
        )

    loads = [
        pltpu.make_async_copy(counts_ref, cnt, load_sem.at[0]),
        pltpu.make_async_copy(colmat_ref, wcol, load_sem.at[1]),
        pltpu.make_async_copy(rowmat_ref, brow_f, load_sem.at[2]),
    ]
    for load in loads:
        load.start()

    ylow[:, ext:, :] = jnp.zeros((slab, 16, columns), bf16)
    hconv[...] = jnp.zeros(hconv.shape, f32)

    @pl.when(jnp.logical_not(has_prev))
    def _():
        halo[0] = jnp.zeros(halo.shape[1:], jnp.int32)

    @pl.when(jnp.logical_not(has_next))
    def _():
        halo[1] = jnp.zeros(halo.shape[1:], jnp.int32)

    @pl.when(jnp.logical_not(has_front))
    def _():
        ufield[0:5] = jnp.zeros((5, ext, columns), f32)
        pack_in[0] = jnp.zeros(pack_in.shape[1:], f32)

    @pl.when(jnp.logical_not(has_back))
    def _():
        ufield[slab + 5 :] = jnp.zeros((5, ext, columns), f32)
        pack_in[1] = jnp.zeros(pack_in.shape[1:], f32)

    for load in loads:
        load.wait()

    for group in range(slab // 8):
        for r in range(5):
            stage[0, group, r] = cnt[group * 8 : group * 8 + 8, r, :]
            stage[1, group, r] = cnt[group * 8 : group * 8 + 8, rows - 5 + r, :]

    row_id = lax.broadcasted_iota(jnp.int32, brow_f.shape, 0)
    outside = ((row_id == 7) & (img == 0)) | ((row_id == rows + 8) & (img == img_count - 1))
    brow[...] = jnp.where(outside, 0.0, brow_f[...]).astype(bf16)

    pl.semaphore_wait(barrier, depth_count + 1)

    def img_copy(side, group):
        target = lax.rem(img + (img_count - 1 if side == 0 else 1), img_count)
        return pltpu.make_async_remote_copy(
            src_ref=stage.at[side, group],
            dst_ref=halo.at[1 - side, group],
            send_sem=img_send.at[side, group],
            recv_sem=img_recv.at[1 - side, group],
            device_id=(target, dep),
            device_id_type=MESH,
        )

    groups = slab // 8
    order = [0, groups - 1] + list(range(1, groups - 1))
    for group in order:
        for side, exists in ((0, has_prev), (1, has_next)):
            @pl.when(exists)
            def _():
                img_copy(side, group).start()

    def column_smooth(block):
        block = block.astype(f32).astype(bf16)
        return jnp.dot(block, wcol[0], preferred_element_type=f32) + jnp.dot(
            block, wcol[1], preferred_element_type=f32
        )

    def halves(value):
        high = value.astype(bf16)
        return high, (value - high.astype(f32)).astype(bf16)

    def own_columns(step, carry):
        at = pl.ds(step * 4, 4)
        smooth = column_smooth(cnt[at].reshape(4 * rows, columns))
        high, low = halves(smooth)
        yhigh[at, :rows, :] = high.reshape(4, rows, columns)
        ylow[at, :rows, :] = low.reshape(4, rows, columns)
        return carry

    lax.fori_loop(0, slab // 4, own_columns, 0)

    def rows_of_group(group):
        for side, exists in ((0, has_prev), (1, has_next)):
            @pl.when(exists)
            def _():
                img_copy(1 - side, group).wait_recv()

        for side in range(2):
            smooth = column_smooth(halo[side, group].reshape(40, columns))
            for r in range(5):
                hconv[:, side * 8 + r, :] = smooth[r * 8 : r * 8 + 8]

        def one_layer(j, carry):
            layer = group * 8 + j
            high, low = halves(hconv[j])
            yhigh[layer, rows:ext, :] = high
            ylow[layer, rows:ext, :] = low
            tall = yhigh[layer]
            field = jnp.concatenate([tall, tall, ylow[layer]], axis=0)
            ufield[layer + 5] = jnp.dot(brow[...], field, preferred_element_type=f32)
            return carry

        lax.fori_loop(0, 8, one_layer, 0)

    def depth_copies(side):
        target = lax.rem(dep + (depth_count - 1 if side == 0 else 1), depth_count)
        source = 5 if side == 0 else slab
        place = slab + 5 if side == 0 else 0
        big = pltpu.make_async_remote_copy(
            src_ref=ufield.at[source : source + 5, 8 : rows + 8, :],
            dst_ref=ufield.at[place : place + 5, 8 : rows + 8, :],
            send_sem=dep_send.at[side, 0],
            recv_sem=dep_recv.at[1 - side, 0],
            device_id=(img, target),
            device_id_type=MESH,
        )
        small = pltpu.make_async_remote_copy(
            src_ref=pack.at[side],
            dst_ref=pack_in.at[1 - side],
            send_sem=dep_send.at[side, 1],
            recv_sem=dep_recv.at[1 - side, 1],
            device_id=(img, target),
            device_id_type=MESH,
        )
        return big, small

    def send_depth(side, exists):
        first = 5 if side == 0 else slab + 1
        for j in range(4):
            pack[side, j : j + 1] = ufield[first + j, 7:8, :]
            pack[side, 4 + j : 5 + j] = ufield[first + j, rows + 8 : rows + 9, :]

        @pl.when(exists)
        def _():
            for copy in depth_copies(side):
                copy.start()

    rows_of_group(0)
    send_depth(0, has_front)
    rows_of_group(groups - 1)
    send_depth(1, has_back)
    for group in range(1, groups - 1):
        rows_of_group(group)

    def depth_smooth(low, high):
        def one_tile(tile, carry):
            r = pl.ds(pl.multiple_of(lax.div(tile, columns // 128) * 8, 8), 8)
            c = pl.ds(pl.multiple_of(lax.rem(tile, columns // 128) * 128, 128), 128)
            held = [ufield[m, r, c] for m in range(low, low + 8)]
            for m in range(low, high):
                held.append(ufield[m + 8, r, c])
                total = gauss_taps[4] * held[4]
                for k in range(4):
                    total = total + gauss_taps[k] * (held[k] + held[8 - k])
                sfield[m, r, c] = total
                held.pop(0)
            return carry

        lax.fori_loop(0, (ext // 8) * (columns // 128), one_tile, 0)

    column_id = lax.broadcasted_iota(jnp.int32, (8, columns), 1)
    at_left, at_right = column_id == 0, column_id == columns - 1

    def shade_layer(layer, tile, state):
        seen, total, red, green = state
        base = 8 + 8 * tile
        here = sfield[layer + 1, base : base + 8, :]
        dz = sfield[layer + 2, base : base + 8, :] - sfield[layer, base : base + 8, :]
        dx = sfield[layer + 1, base + 1 : base + 9, :] - sfield[layer + 1, base - 1 : base + 7, :]
        left = jnp.where(at_left, 0.0, pltpu.roll(here, 1, 1))
        right = jnp.where(at_right, 0.0, pltpu.roll(here, columns - 1, 1))
        dy = right - left
        shading = 0.55 + 0.45 * jnp.tanh(0.72 * dz + 0.9 * dx + 0.96 * dy)
        square = here * here
        bend = dz * dz + dx * dx + dy * dy
        tau = (square * pl.reciprocal(1.0 + square)) * ((1.0 + bend) * (1.5 / depth_total))
        weight = seen * (1.0 - jnp.exp(-tau))
        light = weight * shading
        centred = here - 2.5
        return (
            seen - weight,
            total + light,
            red + light * jnp.tanh(centred),
            green + light * jnp.exp(-(centred * centred)),
        )

    depth_smooth(5, slab - 3)
    zeros = jnp.zeros((8, columns), f32)
    ones = jnp.ones((8, columns), f32)
    for tile in range(tiles):
        state = lax.fori_loop(
            5,
            slab - 5,
            lambda layer, state: shade_layer(layer, tile, state),
            (ones, zeros, zeros, zeros),
            unroll=11,
        )
        for part in range(4):
            partial[part, tile] = state[part]

    for side, exists in ((1, has_back), (0, has_front)):
        @pl.when(exists)
        def _():
            for copy in depth_copies(1 - side):
                copy.wait_recv()

    for j in range(4):
        ufield[1 + j, 7:8, :] = pack_in[0, j : j + 1]
        ufield[1 + j, rows + 8 : rows + 9, :] = pack_in[0, 4 + j : 5 + j]
        ufield[slab + 5 + j, 7:8, :] = pack_in[1, j : j + 1]
        ufield[slab + 5 + j, rows + 8 : rows + 9, :] = pack_in[1, 4 + j : 5 + j]

    depth_smooth(0, 5)
    depth_smooth(slab - 3, slab + 2)

    @pl.when(jnp.logical_not(has_front))
    def _():
        sfield[0] = jnp.zeros((ext, columns), f32)

    @pl.when(jnp.logical_not(has_back))
    def _():
        sfield[slab + 1] = jnp.zeros((ext, columns), f32)

    def all_copy(target, source):
        return pltpu.make_async_remote_copy(
            src_ref=outbox.at[target],
            dst_ref=inbox.at[source],
            send_sem=all_send.at[target],
            recv_sem=all_recv.at[source],
            device_id=(img, target),
            device_id_type=MESH,
        )

    top_half = lax.broadcasted_iota(jnp.int32, (8, columns), 0) < 4
    for tile in range(tiles):
        state = lax.fori_loop(
            0,
            5,
            lambda layer, state: shade_layer(layer, tile, state),
            (ones, zeros, zeros, zeros),
            unroll=5,
        )
        seen = state[0]
        state = (seen * partial[0, tile],) + tuple(
            state[part] + seen * partial[part, tile] for part in range(1, 4)
        )
        seen, total, red, green = lax.fori_loop(
            slab - 5,
            slab,
            lambda layer, state: shade_layer(layer, tile, state),
            state,
            unroll=5,
        )
        outbox[2 * tile, 0:8] = jnp.where(top_half, total, pltpu.roll(red, 4, 0))
        outbox[2 * tile, 8:16] = jnp.where(top_half, green, pltpu.roll(seen, 4, 0))
        outbox[2 * tile + 1, 0:8] = jnp.where(top_half, pltpu.roll(total, 4, 0), red)
        outbox[2 * tile + 1, 8:16] = jnp.where(top_half, pltpu.roll(green, 4, 0), seen)
        for target in (2 * tile, 2 * tile + 1):
            @pl.when(dep != target)
            def _():
                all_copy(target, dep).start()

            @pl.when(dep == target)
            def _():
                inbox[target] = outbox[target]

    def compose(source, state):
        seen, upper, lower = state

        @pl.when(source != dep)
        def _():
            all_copy(source, source).wait_recv()

        first, second = inbox[source, 0:8, :], inbox[source, 8:16, :]
        through = jnp.where(top_half, pltpu.roll(second, 4, 0), second)
        return seen * through, upper + seen * first, lower + seen * second

    seen, upper, lower = lax.fori_loop(0, depth_count, compose, (ones, zeros, zeros))
    total, red = upper[0:4], upper[4:8]
    out_ref[0] = 0.5 * (total + red)
    out_ref[1] = lower[0:4]
    out_ref[2] = 0.5 * (total - red)
    out_ref[3] = 1.0 - seen[0:4]

    for group in range(groups):
        for side, exists in ((0, has_prev), (1, has_next)):
            @pl.when(exists)
            def _():
                img_copy(side, group).wait_send()

    for side, exists in ((0, has_front), (1, has_back)):
        @pl.when(exists)
        def _():
            for copy in depth_copies(side):
                copy.wait_send()

    def finish(target, carry):
        @pl.when(target != dep)
        def _():
            all_copy(target, target).wait_send()

        return carry

    lax.fori_loop(0, depth_count, finish, 0)


def solution(mesh):
    img_count, depth_count = mesh.shape["img"], mesh.shape["depth"]

    def local(counts):
        slab, rows, columns = counts.shape
        ext = rows + 16
        groups = slab // 8

        def body(*refs):
            render_kernel(slab * depth_count, img_count, depth_count, *refs)

        anywhere = pl.BlockSpec(memory_space=pl.ANY)
        return pl.pallas_call(
            body,
            out_shape=jax.ShapeDtypeStruct((4, rows // depth_count, columns), f32),
            in_specs=[anywhere] * 3,
            out_specs=pl.BlockSpec(memory_space=pltpu.VMEM),
            scratch_shapes=[
                pltpu.VMEM((slab, rows, columns), jnp.int32),
                pltpu.VMEM((2, columns, columns), bf16),
                pltpu.VMEM((ext, 3 * ext + 16), f32),
                pltpu.VMEM((ext, 3 * ext + 16), bf16),
                pltpu.VMEM((2, groups, 5, 8, columns), jnp.int32),
                pltpu.VMEM((2, groups, 5, 8, columns), jnp.int32),
                pltpu.VMEM((8, 16, columns), f32),
                pltpu.VMEM((slab, ext, columns), bf16),
                pltpu.VMEM((slab, ext + 16, columns), bf16),
                pltpu.VMEM((slab + 10, ext, columns), f32),
                pltpu.VMEM((slab + 2, ext, columns), f32),
                pltpu.VMEM((2, 8, columns), f32),
                pltpu.VMEM((2, 8, columns), f32),
                pltpu.VMEM((4, rows // 8, 8, columns), f32),
                pltpu.VMEM((depth_count, 16, columns), f32),
                pltpu.VMEM((depth_count, 16, columns), f32),
                pltpu.SemaphoreType.DMA((3,)),
                pltpu.SemaphoreType.DMA((2, groups)),
                pltpu.SemaphoreType.DMA((2, groups)),
                pltpu.SemaphoreType.DMA((2, 2)),
                pltpu.SemaphoreType.DMA((2, 2)),
                pltpu.SemaphoreType.DMA((depth_count,)),
                pltpu.SemaphoreType.DMA((depth_count,)),
            ],
            compiler_params=pltpu.CompilerParams(
                collective_id=0, has_side_effects=True, vmem_limit_bytes=56 << 20
            ),
        )(counts, jnp.asarray(column_matrix(columns)), jnp.asarray(row_matrix(rows)))

    return jax.shard_map(
        local,
        mesh=mesh,
        in_specs=(P("depth", "img", None),),
        out_specs=P(None, ("img", "depth"), None),
        check_vma=False,
    )
```

```python
import math

import jax
import jax.numpy as jnp
import numpy as np
from jax import lax
from jax.experimental import pallas as pl
from jax.experimental.pallas import tpu as pltpu
from jax.sharding import PartitionSpec as P
import ml_dtypes

gauss_taps = [
    math.exp(-offset * offset / 8.0)
    / sum((math.exp(-other * other / 8.0) for other in range(-4, 5)))
    for offset in range(-4, 5)
]
MESH = pl.DeviceIdType.MESH
f32 = jnp.float32
bf16 = jnp.bfloat16
run = 4


def split_taps(matrix):
    high = matrix.astype(np.float32).astype(ml_dtypes.bfloat16).astype(np.float64)
    low = (matrix - high).astype(np.float32).astype(ml_dtypes.bfloat16).astype(np.float64)
    return high, low


def column_matrix(columns):
    index = np.arange(columns)
    offset = index[:, None] - index[None, :]
    matrix = np.zeros((columns, columns))
    for k in range(-4, 5):
        matrix[offset == k] = gauss_taps[k + 4]
    high, low = split_taps(matrix)
    return np.stack([high, low]).astype(ml_dtypes.bfloat16)


def row_matrix(rows):
    target = np.full((rows + 16,), 10**6)
    target[7 : rows + 9] = np.arange(-1, rows + 1)
    source = np.full((rows + 16,), -(10**6))
    source[:rows] = np.arange(rows)
    source[rows : rows + 5] = np.arange(-5, 0)
    source[rows + 8 : rows + 13] = np.arange(rows, rows + 5)
    offset = source[None, :] - target[:, None]
    matrix = np.zeros(offset.shape)
    for k in range(-4, 5):
        matrix[offset == k] = gauss_taps[k + 4]
    high, low = split_taps(matrix)
    pad = np.zeros((rows + 16, 16))
    return np.concatenate([high, low, high, pad], axis=1).astype(np.float32)


def render_kernel(
    depth_total, img_count, depth_count,
    counts_ref, colmat_ref, rowmat_ref, out_ref,
    cnt, wcol, brow_f, brow, stage, halo, hconv, yhigh, ylow, ufield, sfield,
    pack, pack_in, partial, outbox, inbox,
    relay, load_sem, img_send, img_recv, dep_send, dep_recv, all_send, all_recv,
    relay_send, relay_recv,
):
    img = lax.axis_index("img")
    dep = lax.axis_index("depth")
    slab, rows, columns = cnt.shape
    tiles = rows // 8
    owned = rows // depth_count
    ext = rows + 16
    chunks = dep_send.shape[1] - 1
    chunk_rows = rows // chunks

    barrier = pltpu.get_barrier_semaphore()
    has_prev, has_next = img > 0, img < img_count - 1
    has_front, has_back = dep > 0, dep < depth_count - 1

    def greet_depth(step, carry):
        target = lax.rem(dep + step, depth_count)
        pl.semaphore_signal(barrier, inc=1, device_id=(img, target), device_id_type=MESH)
        return carry

    lax.fori_loop(1, depth_count, greet_depth, 0)
    for step in (1, img_count - 1):
        pl.semaphore_signal(
            barrier, inc=1, device_id=(lax.rem(img + step, img_count), dep), device_id_type=MESH
        )

    def load_rows(start, size, sem):
        span = pl.ds(start, size)
        return pltpu.make_async_copy(counts_ref.at[:, span, :], cnt.at[:, span, :], sem)

    loads = [
        load_rows(0, 8, load_sem.at[0]),
        load_rows(rows - 8, 8, load_sem.at[1]),
        load_rows(8, rows - 16, load_sem.at[2]),
        pltpu.make_async_copy(colmat_ref, wcol, load_sem.at[3]),
        pltpu.make_async_copy(rowmat_ref, brow_f, load_sem.at[4]),
    ]
    for load in loads:
        load.start()

    ylow[:, ext:, :] = jnp.zeros((slab, 16, columns), bf16)
    hconv[...] = jnp.zeros(hconv.shape, f32)

    @pl.when(jnp.logical_not(has_prev))
    def _():
        halo[0] = jnp.zeros(halo.shape[1:], jnp.int32)

    @pl.when(jnp.logical_not(has_next))
    def _():
        halo[1] = jnp.zeros(halo.shape[1:], jnp.int32)

    @pl.when(jnp.logical_not(has_front))
    def _():
        ufield[0:5] = jnp.zeros((5, ext, columns), f32)
        pack_in[0] = jnp.zeros(pack_in.shape[1:], f32)

    @pl.when(jnp.logical_not(has_back))
    def _():
        ufield[slab + 5 :] = jnp.zeros((5, ext, columns), f32)
        pack_in[1] = jnp.zeros(pack_in.shape[1:], f32)

    for load in loads[:2]:
        load.wait()

    for group in range(slab // 8):
        for r in range(5):
            stage[0, group, r] = cnt[group * 8 : group * 8 + 8, r, :]
            stage[1, group, r] = cnt[group * 8 : group * 8 + 8, rows - 5 + r, :]

    pl.semaphore_wait(barrier, depth_count + 1)

    def img_copy(side, group):
        target = lax.rem(img + (img_count - 1 if side == 0 else 1), img_count)
        return pltpu.make_async_remote_copy(
            src_ref=stage.at[side, group],
            dst_ref=halo.at[1 - side, group],
            send_sem=img_send.at[side, group],
            recv_sem=img_recv.at[1 - side, group],
            device_id=(target, dep),
            device_id_type=MESH,
        )

    groups = slab // 8
    order = [0, groups - 1] + list(range(1, groups - 1))
    for group in order:
        for side, exists in ((0, has_prev), (1, has_next)):
            @pl.when(exists)
            def _():
                img_copy(side, group).start()

    for load in loads[2:]:
        load.wait()

    row_id = lax.broadcasted_iota(jnp.int32, brow_f.shape, 0)
    outside = ((row_id == 7) & (img == 0)) | ((row_id == rows + 8) & (img == img_count - 1))
    brow[...] = jnp.where(outside, 0.0, brow_f[...]).astype(bf16)

    def column_smooth(block):
        block = block.astype(f32).astype(bf16)
        return jnp.dot(block, wcol[0], preferred_element_type=f32) + jnp.dot(
            block, wcol[1], preferred_element_type=f32
        )

    def halves(value):
        high = value.astype(bf16)
        return high, (value - high.astype(f32)).astype(bf16)

    def own_columns(step, carry):
        at = pl.ds(step * 4, 4)
        smooth = column_smooth(cnt[at].reshape(4 * rows, columns))
        high, low = halves(smooth)
        yhigh[at, :rows, :] = high.reshape(4, rows, columns)
        ylow[at, :rows, :] = low.reshape(4, rows, columns)
        return carry

    lax.fori_loop(0, slab // 4, own_columns, 0)

    def rows_of_group(group):
        for side, exists in ((0, has_prev), (1, has_next)):
            @pl.when(exists)
            def _():
                img_copy(1 - side, group).wait_recv()

        for side in range(2):
            smooth = column_smooth(halo[side, group].reshape(40, columns))
            for r in range(5):
                hconv[:, side * 8 + r, :] = smooth[r * 8 : r * 8 + 8]

        def one_layer(j, carry):
            layer = group * 8 + j
            high, low = halves(hconv[j])
            yhigh[layer, rows:ext, :] = high
            ylow[layer, rows:ext, :] = low
            tall = yhigh[layer]
            field = jnp.concatenate([tall, tall, ylow[layer]], axis=0)
            ufield[layer + 5] = jnp.dot(brow[...], field, preferred_element_type=f32)
            return carry

        lax.fori_loop(0, 8, one_layer, 0)

    def depth_target(side):
        return lax.rem(dep + (depth_count - 1 if side == 0 else 1), depth_count)

    def depth_copy(side, chunk):
        source = 5 if side == 0 else slab
        place = slab + 5 if side == 0 else 0
        span = pl.ds(8 + chunk * chunk_rows, chunk_rows)
        return pltpu.make_async_remote_copy(
            src_ref=ufield.at[source : source + 5, span, :],
            dst_ref=ufield.at[place : place + 5, span, :],
            send_sem=dep_send.at[side, chunk],
            recv_sem=dep_recv.at[1 - side, chunk],
            device_id=(img, depth_target(side)),
            device_id_type=MESH,
        )

    stretch = lax.div(dep, run)
    relays = depth_count // run - 1

    def goes_round(side, chunk):
        if side == 0:
            return has_front & (lax.rem(dep, run) == 0) & (chunk < relays + 1 - stretch)
        return has_back & (lax.rem(dep, run) == run - 1) & (chunk <= stretch)

    def round_copy(side, chunk):
        source = 5 if side == 0 else slab
        step = depth_count - run if side == 0 else run
        return pltpu.make_async_remote_copy(
            src_ref=ufield.at[source : source + 5, pl.ds(8 + chunk * chunk_rows, chunk_rows), :],
            dst_ref=relay.at[chunk],
            send_sem=dep_send.at[side, chunk],
            recv_sem=relay_recv.at[chunk],
            device_id=(img, lax.rem(dep + step, depth_count)),
            device_id_type=MESH,
        )

    def passes_on(side, chunk):
        if side == 0:
            return (lax.rem(dep, run) == 0) & (chunk < relays - stretch)
        return (lax.rem(dep, run) == run - 1) & (chunk < stretch)

    def pass_copy(side, chunk):
        place = slab + 5 if side == 0 else 0
        step = run - 1 if side == 0 else depth_count - run + 1
        return pltpu.make_async_remote_copy(
            src_ref=relay.at[chunk],
            dst_ref=ufield.at[place : place + 5, pl.ds(8 + chunk * chunk_rows, chunk_rows), :],
            send_sem=relay_send.at[chunk],
            recv_sem=dep_recv.at[1 - side, chunk],
            device_id=(img, lax.rem(dep + step, depth_count)),
            device_id_type=MESH,
        )

    def pass_on(chunk):
        for side in range(2):
            @pl.when(passes_on(side, chunk))
            def _():
                round_copy(side, chunk).wait_recv()
                pass_copy(side, chunk).start()

    def edge_copy(side):
        return pltpu.make_async_remote_copy(
            src_ref=pack.at[side],
            dst_ref=pack_in.at[1 - side],
            send_sem=dep_send.at[side, chunks],
            recv_sem=dep_recv.at[1 - side, chunks],
            device_id=(img, depth_target(side)),
            device_id_type=MESH,
        )

    def pack_edges(side):
        first = 5 if side == 0 else slab + 1
        for j in range(4):
            pack[side, j : j + 1] = ufield[first + j, 7:8, :]
            pack[side, 4 + j : 5 + j] = ufield[first + j, rows + 8 : rows + 9, :]

    faces = ((0, has_front), (1, has_back))

    for side, group in ((0, 0), (1, groups - 1)):
        rows_of_group(group)
        pack_edges(side)

        @pl.when(faces[side][1])
        def _():
            edge_copy(side).start()

        for chunk in range(chunks):
            round_trip = goes_round(side, chunk)

            @pl.when(round_trip)
            def _():
                round_copy(side, chunk).start()

            @pl.when(faces[side][1] & jnp.logical_not(round_trip))
            def _():
                depth_copy(side, chunk).start()

    for group in range(1, groups - 1):
        rows_of_group(group)

    def depth_smooth(low, high, first, last):
        def one_tile(tile, carry):
            r = pl.ds(pl.multiple_of(lax.div(tile, columns // 128) * 8, 8), 8)
            c = pl.ds(pl.multiple_of(lax.rem(tile, columns // 128) * 128, 128), 128)
            held = [ufield[m, r, c] for m in range(low, low + 8)]
            for m in range(low, high):
                held.append(ufield[m + 8, r, c])
                total = gauss_taps[4] * held[4]
                for k in range(4):
                    total = total + gauss_taps[k] * (held[k] + held[8 - k])
                sfield[m, r, c] = total
                held.pop(0)
            return carry

        per_row = columns // 128
        lax.fori_loop(first * per_row, last * per_row, one_tile, 0)

    column_id = lax.broadcasted_iota(jnp.int32, (8, columns), 1)
    at_left, at_right = column_id == 0, column_id == columns - 1

    def shade_layer(layer, tile, state):
        seen, total, red, green = state
        base = 8 + 8 * tile
        here = sfield[layer + 1, base : base + 8, :]
        dz = sfield[layer + 2, base : base + 8, :] - sfield[layer, base : base + 8, :]
        dx = sfield[layer + 1, base + 1 : base + 9, :] - sfield[layer + 1, base - 1 : base + 7, :]
        left = jnp.where(at_left, 0.0, pltpu.roll(here, 1, 1))
        right = jnp.where(at_right, 0.0, pltpu.roll(here, columns - 1, 1))
        dy = right - left
        shading = 0.55 + 0.45 * jnp.tanh(0.72 * dz + 0.9 * dx + 0.96 * dy)
        square = here * here
        bend = dz * dz + dx * dx + dy * dy
        tau = (square * pl.reciprocal(1.0 + square)) * ((1.0 + bend) * (1.5 / depth_total))
        weight = seen * (1.0 - jnp.exp(-tau))
        light = weight * shading
        centred = here - 2.5
        return (
            seen - weight,
            total + light,
            red + light * jnp.tanh(centred),
            green + light * jnp.exp(-(centred * centred)),
        )

    depth_smooth(5, slab - 3, 0, ext // 8)
    zeros = jnp.zeros((8, columns), f32)
    ones = jnp.ones((8, columns), f32)
    for tile in range(tiles):
        state = lax.fori_loop(
            5,
            slab - 5,
            lambda layer, state: shade_layer(layer, tile, state),
            (ones, zeros, zeros, zeros),
            unroll=11,
        )
        for part in range(4):
            partial[part, tile] = state[part]
        if tile % 2 == 0 and tile // 2 < relays:
            pass_on(tile // 2)

    for side, exists in faces:
        @pl.when(exists)
        def _():
            edge_copy(1 - side).wait_recv()

    for j in range(4):
        ufield[1 + j, 7:8, :] = pack_in[0, j : j + 1]
        ufield[1 + j, rows + 8 : rows + 9, :] = pack_in[0, 4 + j : 5 + j]
        ufield[slab + 5 + j, 7:8, :] = pack_in[1, j : j + 1]
        ufield[slab + 5 + j, rows + 8 : rows + 9, :] = pack_in[1, 4 + j : 5 + j]

    def finish_chunk(chunk):
        for side, exists in faces:
            @pl.when(exists)
            def _():
                depth_copy(1 - side, chunk).wait_recv()

        tiles_per = chunk_rows // 8
        first = 1 + chunk * tiles_per if chunk > 0 else 0
        last = 1 + (chunk + 1) * tiles_per if chunk < chunks - 1 else ext // 8
        depth_smooth(0, 5, first, last)
        depth_smooth(slab - 3, slab + 2, first, last)
        span = slice(first * 8, last * 8)

        @pl.when(jnp.logical_not(has_front))
        def _():
            sfield[0, span, :] = jnp.zeros((last * 8 - first * 8, columns), f32)

        @pl.when(jnp.logical_not(has_back))
        def _():
            sfield[slab + 1, span, :] = jnp.zeros((last * 8 - first * 8, columns), f32)

    def all_copy(target, source):
        return pltpu.make_async_remote_copy(
            src_ref=outbox.at[target],
            dst_ref=inbox.at[source],
            send_sem=all_send.at[target],
            recv_sem=all_recv.at[source],
            device_id=(img, target),
            device_id_type=MESH,
        )

    top_half = lax.broadcasted_iota(jnp.int32, (8, columns), 0) < 4
    ready = 0
    for tile in range(tiles):
        while ready < chunks and ready * chunk_rows <= min(8 * tile + 8, rows - 1):
            finish_chunk(ready)
            ready += 1
        state = lax.fori_loop(
            0,
            5,
            lambda layer, state: shade_layer(layer, tile, state),
            (ones, zeros, zeros, zeros),
            unroll=5,
        )
        seen = state[0]
        state = (seen * partial[0, tile],) + tuple(
            state[part] + seen * partial[part, tile] for part in range(1, 4)
        )
        seen, total, red, green = lax.fori_loop(
            slab - 5,
            slab,
            lambda layer, state: shade_layer(layer, tile, state),
            state,
            unroll=5,
        )
        outbox[2 * tile, 0:8] = jnp.where(top_half, total, pltpu.roll(red, 4, 0))
        outbox[2 * tile, 8:16] = jnp.where(top_half, green, pltpu.roll(seen, 4, 0))
        outbox[2 * tile + 1, 0:8] = jnp.where(top_half, pltpu.roll(total, 4, 0), red)
        outbox[2 * tile + 1, 8:16] = jnp.where(top_half, pltpu.roll(green, 4, 0), seen)
        for target in (2 * tile, 2 * tile + 1):
            @pl.when(dep != target)
            def _():
                all_copy(target, dep).start()

            @pl.when(dep == target)
            def _():
                inbox[target] = outbox[target]

    def compose(source, state):
        seen, upper, lower = state

        @pl.when(source != dep)
        def _():
            all_copy(source, source).wait_recv()

        first, second = inbox[source, 0:8, :], inbox[source, 8:16, :]
        through = jnp.where(top_half, pltpu.roll(second, 4, 0), second)
        return seen * through, upper + seen * first, lower + seen * second

    seen, upper, lower = lax.fori_loop(0, depth_count, compose, (ones, zeros, zeros))
    out_ref[0] = upper[0:4]
    out_ref[1] = upper[4:8]
    out_ref[2] = lower[0:4]
    out_ref[3] = seen[0:4]

    for group in range(groups):
        for side, exists in ((0, has_prev), (1, has_next)):
            @pl.when(exists)
            def _():
                img_copy(side, group).wait_send()

    for side, exists in ((0, has_front), (1, has_back)):
        @pl.when(exists)
        def _():
            edge_copy(side).wait_send()
            for chunk in range(chunks):
                depth_copy(side, chunk).wait_send()

    def finish(target, carry):
        @pl.when(target != dep)
        def _():
            all_copy(target, target).wait_send()

        return carry

    lax.fori_loop(0, depth_count, finish, 0)

    for chunk in range(relays):
        for side in range(2):
            @pl.when(passes_on(side, chunk))
            def _():
                pass_copy(side, chunk).wait_send()


def solution(mesh):
    img_count, depth_count = mesh.shape["img"], mesh.shape["depth"]

    def local(counts):
        slab, rows, columns = counts.shape
        ext = rows + 16
        groups = slab // 8

        def body(*refs):
            render_kernel(slab * depth_count, img_count, depth_count, *refs)

        anywhere = pl.BlockSpec(memory_space=pl.ANY)
        layers = pl.pallas_call(
            body,
            out_shape=jax.ShapeDtypeStruct((4, rows // depth_count, columns), f32),
            in_specs=[anywhere] * 3,
            out_specs=pl.BlockSpec(memory_space=pltpu.VMEM),
            scratch_shapes=[
                pltpu.VMEM((slab, rows, columns), jnp.int32),
                pltpu.VMEM((2, columns, columns), bf16),
                pltpu.VMEM((ext, 3 * ext + 16), f32),
                pltpu.VMEM((ext, 3 * ext + 16), bf16),
                pltpu.VMEM((2, groups, 5, 8, columns), jnp.int32),
                pltpu.VMEM((2, groups, 5, 8, columns), jnp.int32),
                pltpu.VMEM((8, 16, columns), f32),
                pltpu.VMEM((slab, ext, columns), bf16),
                pltpu.VMEM((slab, ext + 16, columns), bf16),
                pltpu.VMEM((slab + 10, ext, columns), f32),
                pltpu.VMEM((slab + 2, ext, columns), f32),
                pltpu.VMEM((2, 8, columns), f32),
                pltpu.VMEM((2, 8, columns), f32),
                pltpu.VMEM((4, rows // 8, 8, columns), f32),
                pltpu.VMEM((depth_count, 16, columns), f32),
                pltpu.VMEM((depth_count, 16, columns), f32),
                pltpu.VMEM((depth_count // run, 5, rows * run // depth_count, columns), f32),
                pltpu.SemaphoreType.DMA((5,)),
                pltpu.SemaphoreType.DMA((2, groups)),
                pltpu.SemaphoreType.DMA((2, groups)),
                pltpu.SemaphoreType.DMA((2, depth_count // run + 1)),
                pltpu.SemaphoreType.DMA((2, depth_count // run + 1)),
                pltpu.SemaphoreType.DMA((depth_count,)),
                pltpu.SemaphoreType.DMA((depth_count,)),
                pltpu.SemaphoreType.DMA((depth_count // run,)),
                pltpu.SemaphoreType.DMA((depth_count // run,)),
            ],
            compiler_params=pltpu.CompilerParams(
                collective_id=0, has_side_effects=True, vmem_limit_bytes=56 << 20
            ),
        )(counts, jnp.asarray(column_matrix(columns)), jnp.asarray(row_matrix(rows)))
        total, red, green, seen = (layers[part : part + 1] for part in range(4))
        return jnp.concatenate(
            [0.5 * (total + red), green, 0.5 * (total - red), 1.0 - seen], axis=0
        )

    return jax.shard_map(
        local,
        mesh=mesh,
        in_specs=(P("depth", "img", None),),
        out_specs=P(None, ("img", "depth"), None),
        check_vma=False,
    )
```

```python
import math

import jax
import jax.numpy as jnp
import numpy as np
from jax import lax
from jax.experimental import pallas as pl
from jax.experimental.pallas import tpu as pltpu
from jax.sharding import PartitionSpec as P
import ml_dtypes

gauss_taps = [
    math.exp(-offset * offset / 8.0)
    / sum((math.exp(-other * other / 8.0) for other in range(-4, 5)))
    for offset in range(-4, 5)
]
MESH = pl.DeviceIdType.MESH
f32 = jnp.float32
bf16 = jnp.bfloat16
run = 4
img_run = 4


def split_taps(matrix):
    high = matrix.astype(np.float32).astype(ml_dtypes.bfloat16).astype(np.float64)
    low = (matrix - high).astype(np.float32).astype(ml_dtypes.bfloat16).astype(np.float64)
    return high, low


def column_matrix(columns):
    index = np.arange(columns)
    offset = index[:, None] - index[None, :]
    matrix = np.zeros((columns, columns))
    for k in range(-4, 5):
        matrix[offset == k] = gauss_taps[k + 4]
    high, low = split_taps(matrix)
    return np.stack([high, low]).astype(ml_dtypes.bfloat16)


def row_matrix(rows):
    target = np.full((rows + 16,), 10**6)
    target[7 : rows + 9] = np.arange(-1, rows + 1)
    source = np.full((rows + 16,), -(10**6))
    source[:rows] = np.arange(rows)
    source[rows : rows + 5] = np.arange(-5, 0)
    source[rows + 8 : rows + 13] = np.arange(rows, rows + 5)
    offset = source[None, :] - target[:, None]
    matrix = np.zeros(offset.shape)
    for k in range(-4, 5):
        matrix[offset == k] = gauss_taps[k + 4]
    high, low = split_taps(matrix)
    pad = np.zeros((rows + 16, 16))
    return np.concatenate([high, low, high, pad], axis=1).astype(np.float32)


def render_kernel(
    depth_total, img_count, depth_count,
    counts_ref, colmat_ref, rowmat_ref, out_ref,
    cnt, wcol, brow_f, brow, stage, halo, hconv, yhigh, ylow, ufield, sfield,
    pack, pack_in, partial, outbox, inbox,
    relay, load_sem, img_send, img_recv, dep_send, dep_recv, all_send, all_recv,
    relay_send, relay_recv, img_relay, img_relay_send, img_relay_recv,
):
    img = lax.axis_index("img")
    dep = lax.axis_index("depth")
    slab, rows, columns = cnt.shape
    tiles = rows // 8
    owned = rows // depth_count
    ext = rows + 16
    chunks = dep_send.shape[1] - 1
    chunk_rows = rows // chunks

    barrier = pltpu.get_barrier_semaphore()
    has_prev, has_next = img > 0, img < img_count - 1
    has_front, has_back = dep > 0, dep < depth_count - 1

    def greet_depth(step, carry):
        target = lax.rem(dep + step, depth_count)
        pl.semaphore_signal(barrier, inc=1, device_id=(img, target), device_id_type=MESH)
        return carry

    lax.fori_loop(1, depth_count, greet_depth, 0)
    img_partners = [
        step for near in (1, img_run - 1, img_run) for step in (near, img_count - near)
    ]
    for step in img_partners:
        pl.semaphore_signal(
            barrier, inc=1, device_id=(lax.rem(img + step, img_count), dep), device_id_type=MESH
        )

    def load_rows(start, size, sem):
        span = pl.ds(start, size)
        return pltpu.make_async_copy(counts_ref.at[:, span, :], cnt.at[:, span, :], sem)

    loads = [
        load_rows(0, 8, load_sem.at[0]),
        load_rows(rows - 8, 8, load_sem.at[1]),
        load_rows(8, rows - 16, load_sem.at[2]),
        pltpu.make_async_copy(colmat_ref, wcol, load_sem.at[3]),
        pltpu.make_async_copy(rowmat_ref, brow_f, load_sem.at[4]),
    ]
    for load in loads:
        load.start()

    ylow[:, ext:, :] = jnp.zeros((slab, 16, columns), bf16)
    hconv[...] = jnp.zeros(hconv.shape, f32)

    @pl.when(jnp.logical_not(has_prev))
    def _():
        halo[0] = jnp.zeros(halo.shape[1:], jnp.int32)

    @pl.when(jnp.logical_not(has_next))
    def _():
        halo[1] = jnp.zeros(halo.shape[1:], jnp.int32)

    @pl.when(jnp.logical_not(has_front))
    def _():
        ufield[0:5] = jnp.zeros((5, ext, columns), f32)
        pack_in[0] = jnp.zeros(pack_in.shape[1:], f32)

    @pl.when(jnp.logical_not(has_back))
    def _():
        ufield[slab + 5 :] = jnp.zeros((5, ext, columns), f32)
        pack_in[1] = jnp.zeros(pack_in.shape[1:], f32)

    for load in loads[:2]:
        load.wait()

    for group in range(slab // 8):
        for r in range(5):
            stage[0, group, r] = cnt[group * 8 : group * 8 + 8, r, :]
            stage[1, group, r] = cnt[group * 8 : group * 8 + 8, rows - 5 + r, :]

    pl.semaphore_wait(barrier, depth_count - 1 + len(img_partners))

    def img_copy(side, group):
        target = lax.rem(img + (img_count - 1 if side == 0 else 1), img_count)
        return pltpu.make_async_remote_copy(
            src_ref=stage.at[side, group],
            dst_ref=halo.at[1 - side, group],
            send_sem=img_send.at[side, group],
            recv_sem=img_recv.at[1 - side, group],
            device_id=(target, dep),
            device_id_type=MESH,
        )

    def goes_round_img(side, group):
        if group not in round_groups:
            return False
        return img == (img_run if side == 0 else img_count - 1 - img_run)

    def round_img_copy(side, group):
        return pltpu.make_async_remote_copy(
            src_ref=stage.at[side, group],
            dst_ref=img_relay.at[group - round_groups[0]],
            send_sem=img_send.at[side, group],
            recv_sem=img_relay_recv.at[group - round_groups[0]],
            device_id=(lax.rem(img + (img_count - img_run if side == 0 else img_run), img_count), dep),
            device_id_type=MESH,
        )

    def pass_img_copy(side, group):
        step = img_run - 1 if side == 0 else img_count - img_run + 1
        return pltpu.make_async_remote_copy(
            src_ref=img_relay.at[group - round_groups[0]],
            dst_ref=halo.at[1 - side, group],
            send_sem=img_relay_send.at[group - round_groups[0]],
            recv_sem=img_recv.at[1 - side, group],
            device_id=(lax.rem(img + step, img_count), dep),
            device_id_type=MESH,
        )

    groups = slab // 8
    round_groups = (2,)
    img_relays = ((0, img == 0), (1, img == img_count - 1))
    order = [0, groups - 1] + list(range(1, groups - 1))
    for side in range(2):
        for group in round_groups:
            @pl.when(goes_round_img(side, group))
            def _():
                round_img_copy(side, group).start()

    for group in order:
        for side, exists in ((0, has_prev), (1, has_next)):
            round_trip = goes_round_img(side, group)

            @pl.when(exists & jnp.logical_not(round_trip))
            def _():
                img_copy(side, group).start()


    for load in loads[2:]:
        load.wait()

    row_id = lax.broadcasted_iota(jnp.int32, brow_f.shape, 0)
    outside = ((row_id == 7) & (img == 0)) | ((row_id == rows + 8) & (img == img_count - 1))
    brow[...] = jnp.where(outside, 0.0, brow_f[...]).astype(bf16)

    def column_smooth(block):
        block = block.astype(f32).astype(bf16)
        return jnp.dot(block, wcol[0], preferred_element_type=f32) + jnp.dot(
            block, wcol[1], preferred_element_type=f32
        )

    def halves(value):
        high = value.astype(bf16)
        return high, (value - high.astype(f32)).astype(bf16)

    def own_columns(step, carry):
        at = pl.ds(step * 4, 4)
        smooth = column_smooth(cnt[at].reshape(4 * rows, columns))
        high, low = halves(smooth)
        yhigh[at, :rows, :] = high.reshape(4, rows, columns)
        ylow[at, :rows, :] = low.reshape(4, rows, columns)
        return carry

    lax.fori_loop(0, slab // 4, own_columns, 0)

    for side, relaying in img_relays:
        @pl.when(relaying)
        def _():
            for group in round_groups:
                round_img_copy(side, group).wait_recv()
                pass_img_copy(side, group).start()

    def rows_of_group(group):
        for side, exists in ((0, has_prev), (1, has_next)):
            @pl.when(exists)
            def _():
                img_copy(1 - side, group).wait_recv()

        for side in range(2):
            smooth = column_smooth(halo[side, group].reshape(40, columns))
            for r in range(5):
                hconv[:, side * 8 + r, :] = smooth[r * 8 : r * 8 + 8]

        def one_layer(j, carry):
            layer = group * 8 + j
            high, low = halves(hconv[j])
            yhigh[layer, rows:ext, :] = high
            ylow[layer, rows:ext, :] = low
            tall = yhigh[layer]
            field = jnp.concatenate([tall, tall, ylow[layer]], axis=0)
            ufield[layer + 5] = jnp.dot(brow[...], field, preferred_element_type=f32)
            return carry

        lax.fori_loop(0, 8, one_layer, 0)

    def depth_target(side):
        return lax.rem(dep + (depth_count - 1 if side == 0 else 1), depth_count)

    def depth_copy(side, chunk):
        source = 5 if side == 0 else slab
        place = slab + 5 if side == 0 else 0
        span = pl.ds(8 + chunk * chunk_rows, chunk_rows)
        return pltpu.make_async_remote_copy(
            src_ref=ufield.at[source : source + 5, span, :],
            dst_ref=ufield.at[place : place + 5, span, :],
            send_sem=dep_send.at[side, chunk],
            recv_sem=dep_recv.at[1 - side, chunk],
            device_id=(img, depth_target(side)),
            device_id_type=MESH,
        )

    stretch = lax.div(dep, run)
    relays = depth_count // run - 1

    def goes_round(side, chunk):
        if side == 0:
            return has_front & (lax.rem(dep, run) == 0) & (chunk < relays + 1 - stretch)
        return has_back & (lax.rem(dep, run) == run - 1) & (chunk <= stretch)

    def round_copy(side, chunk):
        source = 5 if side == 0 else slab
        step = depth_count - run if side == 0 else run
        return pltpu.make_async_remote_copy(
            src_ref=ufield.at[source : source + 5, pl.ds(8 + chunk * chunk_rows, chunk_rows), :],
            dst_ref=relay.at[chunk],
            send_sem=dep_send.at[side, chunk],
            recv_sem=relay_recv.at[chunk],
            device_id=(img, lax.rem(dep + step, depth_count)),
            device_id_type=MESH,
        )

    def passes_on(side, chunk):
        if side == 0:
            return (lax.rem(dep, run) == 0) & (chunk < relays - stretch)
        return (lax.rem(dep, run) == run - 1) & (chunk < stretch)

    def pass_copy(side, chunk):
        place = slab + 5 if side == 0 else 0
        step = run - 1 if side == 0 else depth_count - run + 1
        return pltpu.make_async_remote_copy(
            src_ref=relay.at[chunk],
            dst_ref=ufield.at[place : place + 5, pl.ds(8 + chunk * chunk_rows, chunk_rows), :],
            send_sem=relay_send.at[chunk],
            recv_sem=dep_recv.at[1 - side, chunk],
            device_id=(img, lax.rem(dep + step, depth_count)),
            device_id_type=MESH,
        )

    def pass_on(chunk):
        for side in range(2):
            @pl.when(passes_on(side, chunk))
            def _():
                round_copy(side, chunk).wait_recv()
                pass_copy(side, chunk).start()

    def edge_copy(side):
        return pltpu.make_async_remote_copy(
            src_ref=pack.at[side],
            dst_ref=pack_in.at[1 - side],
            send_sem=dep_send.at[side, chunks],
            recv_sem=dep_recv.at[1 - side, chunks],
            device_id=(img, depth_target(side)),
            device_id_type=MESH,
        )

    def pack_edges(side):
        first = 5 if side == 0 else slab + 1
        for j in range(4):
            pack[side, j : j + 1] = ufield[first + j, 7:8, :]
            pack[side, 4 + j : 5 + j] = ufield[first + j, rows + 8 : rows + 9, :]

    faces = ((0, has_front), (1, has_back))

    for side, group in ((0, 0), (1, groups - 1)):
        rows_of_group(group)
        pack_edges(side)

        @pl.when(faces[side][1])
        def _():
            edge_copy(side).start()

        for chunk in range(chunks):
            round_trip = goes_round(side, chunk)

            @pl.when(round_trip)
            def _():
                round_copy(side, chunk).start()

            @pl.when(faces[side][1] & jnp.logical_not(round_trip))
            def _():
                depth_copy(side, chunk).start()

    for group in range(1, groups - 1):
        rows_of_group(group)

    def depth_smooth(low, high, first, last):
        def one_tile(tile, carry):
            r = pl.ds(pl.multiple_of(lax.div(tile, columns // 128) * 8, 8), 8)
            c = pl.ds(pl.multiple_of(lax.rem(tile, columns // 128) * 128, 128), 128)
            held = [ufield[m, r, c] for m in range(low, low + 8)]
            for m in range(low, high):
                held.append(ufield[m + 8, r, c])
                total = gauss_taps[4] * held[4]
                for k in range(4):
                    total = total + gauss_taps[k] * (held[k] + held[8 - k])
                sfield[m, r, c] = total
                held.pop(0)
            return carry

        per_row = columns // 128
        lax.fori_loop(first * per_row, last * per_row, one_tile, 0)

    column_id = lax.broadcasted_iota(jnp.int32, (8, columns), 1)
    at_left, at_right = column_id == 0, column_id == columns - 1
    row_in_tile = lax.broadcasted_iota(jnp.int32, (8, columns), 0)
    is_first_row, is_last_row = row_in_tile == 0, row_in_tile == 7

    def shade_layer(layer, tile, state):
        seen, total, red, green = state
        base = pl.multiple_of(8 + 8 * tile, 8)
        span = pl.ds(base, 8)
        here = sfield[layer + 1, span, :]
        dz = sfield[layer + 2, span, :] - sfield[layer, span, :]
        above = sfield[layer + 1, pl.ds(pl.multiple_of(8 * tile, 8), 8), :]
        below = sfield[layer + 1, pl.ds(pl.multiple_of(16 + 8 * tile, 8), 8), :]
        before = pltpu.roll(jnp.where(is_last_row, above, here), 1, 0)
        after = pltpu.roll(jnp.where(is_first_row, below, here), 7, 0)
        dx = after - before
        left = jnp.where(at_left, 0.0, pltpu.roll(here, 1, 1))
        right = jnp.where(at_right, 0.0, pltpu.roll(here, columns - 1, 1))
        dy = right - left
        shading = 0.55 + 0.45 * jnp.tanh(0.72 * dz + 0.9 * dx + 0.96 * dy)
        square = here * here
        bend = dz * dz + dx * dx + dy * dy
        tau = (square * pl.reciprocal(1.0 + square)) * ((1.0 + bend) * (1.5 / depth_total))
        weight = seen * (1.0 - jnp.exp(-tau))
        light = weight * shading
        centred = here - 2.5
        return (
            seen - weight,
            total + light,
            red + light * jnp.tanh(centred),
            green + light * jnp.exp(-(centred * centred)),
        )

    depth_smooth(5, slab - 3, 0, ext // 8)
    zeros = jnp.zeros((8, columns), f32)
    ones = jnp.ones((8, columns), f32)
    def shade_layers(first, last, tile, state):
        return lax.fori_loop(
            first,
            last,
            lambda layer, state: shade_layer(layer, tile, state),
            state,
            unroll=min(last - first, 11),
        )

    def inner_tile(tile, carry):
        state = shade_layers(5, slab - 5, tile, (ones, zeros, zeros, zeros))
        for part in range(4):
            partial[part, tile] = state[part]
        return carry

    for chunk in range(relays):
        lax.fori_loop(chunk * 2, chunk * 2 + 2, inner_tile, 0)
        pass_on(chunk)
    lax.fori_loop(relays * 2, tiles, inner_tile, 0)

    for side, exists in faces:
        @pl.when(exists)
        def _():
            edge_copy(1 - side).wait_recv()

    for j in range(4):
        ufield[1 + j, 7:8, :] = pack_in[0, j : j + 1]
        ufield[1 + j, rows + 8 : rows + 9, :] = pack_in[0, 4 + j : 5 + j]
        ufield[slab + 5 + j, 7:8, :] = pack_in[1, j : j + 1]
        ufield[slab + 5 + j, rows + 8 : rows + 9, :] = pack_in[1, 4 + j : 5 + j]

    def finish_chunk(chunk):
        for side, exists in faces:
            @pl.when(exists)
            def _():
                depth_copy(1 - side, chunk).wait_recv()

        tiles_per = chunk_rows // 8
        first = 1 + chunk * tiles_per if chunk > 0 else 0
        last = 1 + (chunk + 1) * tiles_per if chunk < chunks - 1 else ext // 8
        depth_smooth(0, 5, first, last)
        depth_smooth(slab - 3, slab + 2, first, last)
        span = slice(first * 8, last * 8)

        @pl.when(jnp.logical_not(has_front))
        def _():
            sfield[0, span, :] = jnp.zeros((last * 8 - first * 8, columns), f32)

        @pl.when(jnp.logical_not(has_back))
        def _():
            sfield[slab + 1, span, :] = jnp.zeros((last * 8 - first * 8, columns), f32)

    def all_copy(target, source):
        return pltpu.make_async_remote_copy(
            src_ref=outbox.at[target],
            dst_ref=inbox.at[source],
            send_sem=all_send.at[target],
            recv_sem=all_recv.at[source],
            device_id=(img, target),
            device_id_type=MESH,
        )

    top_half = row_in_tile < 4
    def outer_tile(tile, carry):
        state = shade_layers(0, 5, tile, (ones, zeros, zeros, zeros))
        seen = state[0]
        state = (seen * partial[0, tile],) + tuple(
            state[part] + seen * partial[part, tile] for part in range(1, 4)
        )
        seen, total, red, green = shade_layers(slab - 5, slab, tile, state)
        outbox[2 * tile, 0:8] = jnp.where(top_half, total, pltpu.roll(red, 4, 0))
        outbox[2 * tile, 8:16] = jnp.where(top_half, green, pltpu.roll(seen, 4, 0))
        outbox[2 * tile + 1, 0:8] = jnp.where(top_half, pltpu.roll(total, 4, 0), red)
        outbox[2 * tile + 1, 8:16] = jnp.where(top_half, pltpu.roll(green, 4, 0), seen)
        for target in (2 * tile, 2 * tile + 1):
            @pl.when(dep != target)
            def _():
                all_copy(target, dep).start()

            @pl.when(dep == target)
            def _():
                inbox[target] = outbox[target]

        return carry

    begun = 0
    for chunk in range(chunks):
        finish_chunk(chunk)
        done = tiles if chunk == chunks - 1 else (chunk + 1) * (chunk_rows // 8) - 1
        lax.fori_loop(begun, done, outer_tile, 0)
        begun = done

    def compose(source, state):
        seen, upper, lower = state

        @pl.when(source != dep)
        def _():
            all_copy(source, source).wait_recv()

        first, second = inbox[source, 0:8, :], inbox[source, 8:16, :]
        through = jnp.where(top_half, pltpu.roll(second, 4, 0), second)
        return seen * through, upper + seen * first, lower + seen * second

    seen, upper, lower = lax.fori_loop(0, depth_count, compose, (ones, zeros, zeros))
    total, red = upper[0:4], upper[4:8]
    out_ref[0] = -0.5 * (total + red)
    out_ref[1] = -lower[0:4]
    out_ref[2] = -0.5 * (total - red)
    out_ref[3] = seen[0:4] - 1.0

    for group in range(groups):
        for side, exists in ((0, has_prev), (1, has_next)):
            @pl.when(exists)
            def _():
                img_copy(side, group).wait_send()

    for side, exists in ((0, has_front), (1, has_back)):
        @pl.when(exists)
        def _():
            edge_copy(side).wait_send()
            for chunk in range(chunks):
                depth_copy(side, chunk).wait_send()

    def finish(target, carry):
        @pl.when(target != dep)
        def _():
            all_copy(target, target).wait_send()

        return carry

    lax.fori_loop(0, depth_count, finish, 0)

    for chunk in range(relays):
        for side in range(2):
            @pl.when(passes_on(side, chunk))
            def _():
                pass_copy(side, chunk).wait_send()

    for side, relaying in img_relays:
        @pl.when(relaying)
        def _():
            for group in round_groups:
                pass_img_copy(side, group).wait_send()


def solution(mesh):
    img_count, depth_count = mesh.shape["img"], mesh.shape["depth"]

    def local(counts):
        slab, rows, columns = counts.shape
        ext = rows + 16
        groups = slab // 8

        def body(*refs):
            render_kernel(slab * depth_count, img_count, depth_count, *refs)

        anywhere = pl.BlockSpec(memory_space=pl.ANY)
        layers = pl.pallas_call(
            body,
            out_shape=jax.ShapeDtypeStruct((4, rows // depth_count, columns), f32),
            in_specs=[anywhere] * 3,
            out_specs=pl.BlockSpec(memory_space=pltpu.VMEM),
            scratch_shapes=[
                pltpu.VMEM((slab, rows, columns), jnp.int32),
                pltpu.VMEM((2, columns, columns), bf16),
                pltpu.VMEM((ext, 3 * ext + 16), f32),
                pltpu.VMEM((ext, 3 * ext + 16), bf16),
                pltpu.VMEM((2, groups, 5, 8, columns), jnp.int32),
                pltpu.VMEM((2, groups, 5, 8, columns), jnp.int32),
                pltpu.VMEM((8, 16, columns), f32),
                pltpu.VMEM((slab, ext, columns), bf16),
                pltpu.VMEM((slab, ext + 16, columns), bf16),
                pltpu.VMEM((slab + 10, ext, columns), f32),
                pltpu.VMEM((slab + 2, ext, columns), f32),
                pltpu.VMEM((2, 8, columns), f32),
                pltpu.VMEM((2, 8, columns), f32),
                pltpu.VMEM((4, rows // 8, 8, columns), f32),
                pltpu.VMEM((depth_count, 16, columns), f32),
                pltpu.VMEM((depth_count, 16, columns), f32),
                pltpu.VMEM((depth_count // run, 5, rows * run // depth_count, columns), f32),
                pltpu.SemaphoreType.DMA((5,)),
                pltpu.SemaphoreType.DMA((2, groups)),
                pltpu.SemaphoreType.DMA((2, groups)),
                pltpu.SemaphoreType.DMA((2, depth_count // run + 1)),
                pltpu.SemaphoreType.DMA((2, depth_count // run + 1)),
                pltpu.SemaphoreType.DMA((depth_count,)),
                pltpu.SemaphoreType.DMA((depth_count,)),
                pltpu.SemaphoreType.DMA((depth_count // run,)),
                pltpu.SemaphoreType.DMA((depth_count // run,)),
                pltpu.VMEM((2, 5, 8, columns), jnp.int32),
                pltpu.SemaphoreType.DMA((2,)),
                pltpu.SemaphoreType.DMA((2,)),
            ],
            compiler_params=pltpu.CompilerParams(
                collective_id=0, has_side_effects=True, vmem_limit_bytes=56 << 20
            ),
        )(counts, jnp.asarray(column_matrix(columns)), jnp.asarray(row_matrix(rows)))
        return -layers

    return jax.shard_map(
        local,
        mesh=mesh,
        in_specs=(P("depth", "img", None),),
        out_specs=P(None, ("img", "depth"), None),
        check_vma=False,
    )
```

```python
import math

import jax
import jax.numpy as jnp
import numpy as np
from jax import lax
from jax.experimental import pallas as pl
from jax.experimental.pallas import tpu as pltpu
from jax.sharding import PartitionSpec as P
import ml_dtypes

gauss_taps = [
    math.exp(-offset * offset / 8.0)
    / sum((math.exp(-other * other / 8.0) for other in range(-4, 5)))
    for offset in range(-4, 5)
]
MESH = pl.DeviceIdType.MESH
f32 = jnp.float32
bf16 = jnp.bfloat16
run = 4
img_run = 4


def split_taps(matrix):
    high = matrix.astype(np.float32).astype(ml_dtypes.bfloat16).astype(np.float64)
    low = (matrix - high).astype(np.float32).astype(ml_dtypes.bfloat16).astype(np.float64)
    return high, low


def column_matrix(columns):
    index = np.arange(columns)
    offset = index[:, None] - index[None, :]
    matrix = np.zeros((columns, columns))
    for k in range(-4, 5):
        matrix[offset == k] = gauss_taps[k + 4]
    high, low = split_taps(matrix)
    return np.stack([high, low]).astype(ml_dtypes.bfloat16)


def row_matrix(rows):
    target = np.full((rows + 16,), 10**6)
    target[7 : rows + 9] = np.arange(-1, rows + 1)
    source = np.full((rows + 16,), -(10**6))
    source[:rows] = np.arange(rows)
    source[rows : rows + 5] = np.arange(-5, 0)
    source[rows + 8 : rows + 13] = np.arange(rows, rows + 5)
    offset = source[None, :] - target[:, None]
    matrix = np.zeros(offset.shape)
    for k in range(-4, 5):
        matrix[offset == k] = gauss_taps[k + 4]
    high, low = split_taps(matrix)
    pad = np.zeros((rows + 16, 16))
    return np.concatenate([high, low, high, pad], axis=1).astype(np.float32)


def render_kernel(
    depth_total, img_count, depth_count,
    counts_ref, colmat_ref, rowmat_ref, out_ref,
    cnt, wcol, brow_f, brow, stage, halo, hconv, yhigh, ylow, ufield, sfield,
    pack, pack_in, partial, outbox, inbox,
    relay, load_sem, img_send, img_recv, dep_send, dep_recv, all_send, all_recv,
    relay_send, relay_recv, img_relay, img_relay_send, img_relay_recv,
):
    img = lax.axis_index("img")
    dep = lax.axis_index("depth")
    slab, rows, columns = cnt.shape
    tiles = rows // 8
    owned = rows // depth_count
    ext = rows + 16
    chunks = dep_send.shape[1] - 1
    chunk_rows = rows // chunks

    barrier = pltpu.get_barrier_semaphore()
    has_prev, has_next = img > 0, img < img_count - 1
    has_front, has_back = dep > 0, dep < depth_count - 1

    def greet_depth(step, carry):
        target = lax.rem(dep + step, depth_count)
        pl.semaphore_signal(barrier, inc=1, device_id=(img, target), device_id_type=MESH)
        return carry

    lax.fori_loop(1, depth_count, greet_depth, 0)
    img_partners = [
        step for near in (1, img_run - 1, img_run) for step in (near, img_count - near)
    ]
    for step in img_partners:
        pl.semaphore_signal(
            barrier, inc=1, device_id=(lax.rem(img + step, img_count), dep), device_id_type=MESH
        )

    def load_rows(start, size, sem):
        span = pl.ds(start, size)
        return pltpu.make_async_copy(counts_ref.at[:, span, :], cnt.at[:, span, :], sem)

    loads = [
        load_rows(0, 8, load_sem.at[0]),
        load_rows(rows - 8, 8, load_sem.at[1]),
        load_rows(8, rows - 16, load_sem.at[2]),
        pltpu.make_async_copy(colmat_ref, wcol, load_sem.at[3]),
        pltpu.make_async_copy(rowmat_ref, brow_f, load_sem.at[4]),
    ]
    for load in loads:
        load.start()

    ylow[:, ext:, :] = jnp.zeros((slab, 16, columns), bf16)
    hconv[...] = jnp.zeros(hconv.shape, f32)

    @pl.when(jnp.logical_not(has_prev))
    def _():
        halo[0] = jnp.zeros(halo.shape[1:], jnp.int32)

    @pl.when(jnp.logical_not(has_next))
    def _():
        halo[1] = jnp.zeros(halo.shape[1:], jnp.int32)

    @pl.when(jnp.logical_not(has_front))
    def _():
        ufield[0:5] = jnp.zeros((5, ext, columns), f32)
        pack_in[0] = jnp.zeros(pack_in.shape[1:], f32)

    @pl.when(jnp.logical_not(has_back))
    def _():
        ufield[slab + 5 :] = jnp.zeros((5, ext, columns), f32)
        pack_in[1] = jnp.zeros(pack_in.shape[1:], f32)

    for load in loads[:2]:
        load.wait()

    for group in range(slab // 8):
        for r in range(5):
            stage[0, group, r] = cnt[group * 8 : group * 8 + 8, r, :]
            stage[1, group, r] = cnt[group * 8 : group * 8 + 8, rows - 5 + r, :]

    pl.semaphore_wait(barrier, depth_count - 1 + len(img_partners))

    def img_copy(side, group):
        target = lax.rem(img + (img_count - 1 if side == 0 else 1), img_count)
        return pltpu.make_async_remote_copy(
            src_ref=stage.at[side, group],
            dst_ref=halo.at[1 - side, group],
            send_sem=img_send.at[side, group],
            recv_sem=img_recv.at[1 - side, group],
            device_id=(target, dep),
            device_id_type=MESH,
        )

    def goes_round_img(side, group):
        if group not in round_groups:
            return False
        return img == (img_run if side == 0 else img_count - 1 - img_run)

    def round_img_copy(side, group):
        return pltpu.make_async_remote_copy(
            src_ref=stage.at[side, group],
            dst_ref=img_relay.at[group - round_groups[0]],
            send_sem=img_send.at[side, group],
            recv_sem=img_relay_recv.at[group - round_groups[0]],
            device_id=(lax.rem(img + (img_count - img_run if side == 0 else img_run), img_count), dep),
            device_id_type=MESH,
        )

    def pass_img_copy(side, group):
        step = img_run - 1 if side == 0 else img_count - img_run + 1
        return pltpu.make_async_remote_copy(
            src_ref=img_relay.at[group - round_groups[0]],
            dst_ref=halo.at[1 - side, group],
            send_sem=img_relay_send.at[group - round_groups[0]],
            recv_sem=img_recv.at[1 - side, group],
            device_id=(lax.rem(img + step, img_count), dep),
            device_id_type=MESH,
        )

    groups = slab // 8
    round_groups = (2,)
    img_relays = ((0, img == 0), (1, img == img_count - 1))
    order = [0, groups - 1] + list(range(1, groups - 1))
    for side in range(2):
        for group in round_groups:
            @pl.when(goes_round_img(side, group))
            def _():
                round_img_copy(side, group).start()

    for group in order:
        for side, exists in ((0, has_prev), (1, has_next)):
            round_trip = goes_round_img(side, group)

            @pl.when(exists & jnp.logical_not(round_trip))
            def _():
                img_copy(side, group).start()


    for load in loads[2:]:
        load.wait()

    row_id = lax.broadcasted_iota(jnp.int32, brow_f.shape, 0)
    outside = ((row_id == 7) & (img == 0)) | ((row_id == rows + 8) & (img == img_count - 1))
    brow[...] = jnp.where(outside, 0.0, brow_f[...]).astype(bf16)

    def column_smooth(block):
        block = block.astype(f32).astype(bf16)
        return jnp.dot(block, wcol[0], preferred_element_type=f32) + jnp.dot(
            block, wcol[1], preferred_element_type=f32
        )

    def halves(value):
        high = value.astype(bf16)
        return high, (value - high.astype(f32)).astype(bf16)

    def own_columns(step, carry):
        at = pl.ds(step * 4, 4)
        smooth = column_smooth(cnt[at].reshape(4 * rows, columns))
        high, low = halves(smooth)
        yhigh[at, :rows, :] = high.reshape(4, rows, columns)
        ylow[at, :rows, :] = low.reshape(4, rows, columns)
        return carry

    def pass_rows():
        for side, relaying in img_relays:
            @pl.when(relaying)
            def _():
                for group in round_groups:
                    round_img_copy(side, group).wait_recv()
                    pass_img_copy(side, group).start()

    def rows_of_group(group):
        lax.fori_loop(group * 2, group * 2 + 2, own_columns, 0)
        for side, exists in ((0, has_prev), (1, has_next)):
            @pl.when(exists)
            def _():
                img_copy(1 - side, group).wait_recv()

        for side in range(2):
            smooth = column_smooth(halo[side, group].reshape(40, columns))
            for r in range(5):
                hconv[:, side * 8 + r, :] = smooth[r * 8 : r * 8 + 8]

        def one_layer(j, carry):
            layer = group * 8 + j
            high, low = halves(hconv[j])
            yhigh[layer, rows:ext, :] = high
            ylow[layer, rows:ext, :] = low
            tall = yhigh[layer]
            field = jnp.concatenate([tall, tall, ylow[layer]], axis=0)
            ufield[layer + 5] = jnp.dot(brow[...], field, preferred_element_type=f32)
            return carry

        lax.fori_loop(0, 8, one_layer, 0)

    def depth_target(side):
        return lax.rem(dep + (depth_count - 1 if side == 0 else 1), depth_count)

    def depth_copy(side, chunk):
        source = 5 if side == 0 else slab
        place = slab + 5 if side == 0 else 0
        span = pl.ds(8 + chunk * chunk_rows, chunk_rows)
        return pltpu.make_async_remote_copy(
            src_ref=ufield.at[source : source + 5, span, :],
            dst_ref=ufield.at[place : place + 5, span, :],
            send_sem=dep_send.at[side, chunk],
            recv_sem=dep_recv.at[1 - side, chunk],
            device_id=(img, depth_target(side)),
            device_id_type=MESH,
        )

    stretch = lax.div(dep, run)
    relays = depth_count // run - 1

    def goes_round(side, chunk):
        if side == 0:
            return has_front & (lax.rem(dep, run) == 0) & (chunk < relays + 1 - stretch)
        return has_back & (lax.rem(dep, run) == run - 1) & (chunk <= stretch)

    def round_copy(side, chunk):
        source = 5 if side == 0 else slab
        step = depth_count - run if side == 0 else run
        return pltpu.make_async_remote_copy(
            src_ref=ufield.at[source : source + 5, pl.ds(8 + chunk * chunk_rows, chunk_rows), :],
            dst_ref=relay.at[chunk],
            send_sem=dep_send.at[side, chunk],
            recv_sem=relay_recv.at[chunk],
            device_id=(img, lax.rem(dep + step, depth_count)),
            device_id_type=MESH,
        )

    def passes_on(side, chunk):
        if side == 0:
            return (lax.rem(dep, run) == 0) & (chunk < relays - stretch)
        return (lax.rem(dep, run) == run - 1) & (chunk < stretch)

    def pass_copy(side, chunk):
        place = slab + 5 if side == 0 else 0
        step = run - 1 if side == 0 else depth_count - run + 1
        return pltpu.make_async_remote_copy(
            src_ref=relay.at[chunk],
            dst_ref=ufield.at[place : place + 5, pl.ds(8 + chunk * chunk_rows, chunk_rows), :],
            send_sem=relay_send.at[chunk],
            recv_sem=dep_recv.at[1 - side, chunk],
            device_id=(img, lax.rem(dep + step, depth_count)),
            device_id_type=MESH,
        )

    def pass_on(chunk):
        for side in range(2):
            @pl.when(passes_on(side, chunk))
            def _():
                round_copy(side, chunk).wait_recv()
                pass_copy(side, chunk).start()

    def edge_copy(side):
        return pltpu.make_async_remote_copy(
            src_ref=pack.at[side],
            dst_ref=pack_in.at[1 - side],
            send_sem=dep_send.at[side, chunks],
            recv_sem=dep_recv.at[1 - side, chunks],
            device_id=(img, depth_target(side)),
            device_id_type=MESH,
        )

    def pack_edges(side):
        first = 5 if side == 0 else slab + 1
        for j in range(4):
            pack[side, j : j + 1] = ufield[first + j, 7:8, :]
            pack[side, 4 + j : 5 + j] = ufield[first + j, rows + 8 : rows + 9, :]

    faces = ((0, has_front), (1, has_back))

    for side, group in ((0, 0), (1, groups - 1)):
        rows_of_group(group)
        if side == 0:
            pass_rows()
        pack_edges(side)

        @pl.when(faces[side][1])
        def _():
            edge_copy(side).start()

        for chunk in range(chunks):
            round_trip = goes_round(side, chunk)

            @pl.when(round_trip)
            def _():
                round_copy(side, chunk).start()

            @pl.when(faces[side][1] & jnp.logical_not(round_trip))
            def _():
                depth_copy(side, chunk).start()

    for group in range(1, groups - 1):
        rows_of_group(group)

    def depth_smooth(low, high, first, last):
        def one_tile(tile, carry):
            r = pl.ds(pl.multiple_of(lax.div(tile, columns // 128) * 8, 8), 8)
            c = pl.ds(pl.multiple_of(lax.rem(tile, columns // 128) * 128, 128), 128)
            held = [ufield[m, r, c] for m in range(low, low + 8)]
            for m in range(low, high):
                held.append(ufield[m + 8, r, c])
                total = gauss_taps[4] * held[4]
                for k in range(4):
                    total = total + gauss_taps[k] * (held[k] + held[8 - k])
                sfield[m, r, c] = total
                held.pop(0)
            return carry

        per_row = columns // 128
        lax.fori_loop(first * per_row, last * per_row, one_tile, 0)

    column_id = lax.broadcasted_iota(jnp.int32, (8, columns), 1)
    at_left, at_right = column_id == 0, column_id == columns - 1
    row_in_tile = lax.broadcasted_iota(jnp.int32, (8, columns), 0)
    is_first_row, is_last_row = row_in_tile == 0, row_in_tile == 7

    def shade_layer(layer, tile, state):
        seen, total, red, green = state
        base = pl.multiple_of(8 + 8 * tile, 8)
        span = pl.ds(base, 8)
        here = sfield[layer + 1, span, :]
        dz = sfield[layer + 2, span, :] - sfield[layer, span, :]
        above = sfield[layer + 1, pl.ds(pl.multiple_of(8 * tile, 8), 8), :]
        below = sfield[layer + 1, pl.ds(pl.multiple_of(16 + 8 * tile, 8), 8), :]
        before = pltpu.roll(jnp.where(is_last_row, above, here), 1, 0)
        after = pltpu.roll(jnp.where(is_first_row, below, here), 7, 0)
        dx = after - before
        left = jnp.where(at_left, 0.0, pltpu.roll(here, 1, 1))
        right = jnp.where(at_right, 0.0, pltpu.roll(here, columns - 1, 1))
        dy = right - left
        shading = 0.55 + 0.45 * jnp.tanh(0.72 * dz + 0.9 * dx + 0.96 * dy)
        square = here * here
        bend = dz * dz + dx * dx + dy * dy
        tau = (square * pl.reciprocal(1.0 + square)) * ((1.0 + bend) * (1.5 / depth_total))
        weight = seen * (1.0 - jnp.exp(-tau))
        light = weight * shading
        centred = here - 2.5
        return (
            seen - weight,
            total + light,
            red + light * jnp.tanh(centred),
            green + light * jnp.exp(-(centred * centred)),
        )

    depth_smooth(5, slab - 3, 0, ext // 8)
    zeros = jnp.zeros((8, columns), f32)
    ones = jnp.ones((8, columns), f32)
    def shade_layers(first, last, tile, state):
        return lax.fori_loop(
            first,
            last,
            lambda layer, state: shade_layer(layer, tile, state),
            state,
            unroll=min(last - first, 11),
        )

    def inner_tile(tile, carry):
        state = shade_layers(5, slab - 5, tile, (ones, zeros, zeros, zeros))
        for part in range(4):
            partial[part, tile] = state[part]
        return carry

    for chunk in range(relays):
        lax.fori_loop(chunk * 2, chunk * 2 + 2, inner_tile, 0)
        pass_on(chunk)
    lax.fori_loop(relays * 2, tiles, inner_tile, 0)

    for side, exists in faces:
        @pl.when(exists)
        def _():
            edge_copy(1 - side).wait_recv()

    for j in range(4):
        ufield[1 + j, 7:8, :] = pack_in[0, j : j + 1]
        ufield[1 + j, rows + 8 : rows + 9, :] = pack_in[0, 4 + j : 5 + j]
        ufield[slab + 5 + j, 7:8, :] = pack_in[1, j : j + 1]
        ufield[slab + 5 + j, rows + 8 : rows + 9, :] = pack_in[1, 4 + j : 5 + j]

    def finish_chunk(side, chunk):
        @pl.when(faces[side][1])
        def _():
            depth_copy(1 - side, chunk).wait_recv()

        tiles_per = chunk_rows // 8
        first = 1 + chunk * tiles_per if chunk > 0 else 0
        last = 1 + (chunk + 1) * tiles_per if chunk < chunks - 1 else ext // 8
        span = slice(first * 8, last * 8)
        if side == 0:
            depth_smooth(0, 5, first, last)
        else:
            depth_smooth(slab - 3, slab + 2, first, last)

        @pl.when(jnp.logical_not(faces[side][1]))
        def _():
            beyond = 0 if side == 0 else slab + 1
            sfield[beyond, span, :] = jnp.zeros((last * 8 - first * 8, columns), f32)

    def all_copy(target, source):
        return pltpu.make_async_remote_copy(
            src_ref=outbox.at[target],
            dst_ref=inbox.at[source],
            send_sem=all_send.at[target],
            recv_sem=all_recv.at[source],
            device_id=(img, target),
            device_id_type=MESH,
        )

    top_half = row_in_tile < 4
    def back_tile(tile, carry):
        state = shade_layers(slab - 5, slab, tile, (ones, zeros, zeros, zeros))
        seen = partial[0, tile]
        for part in range(1, 4):
            partial[part, tile] = partial[part, tile] + seen * state[part]
        partial[0, tile] = seen * state[0]
        return carry

    def outer_tile(tile, carry):
        state = shade_layers(0, 5, tile, (ones, zeros, zeros, zeros))
        total, red, green = (
            state[part] + state[0] * partial[part, tile] for part in range(1, 4)
        )
        seen = state[0] * partial[0, tile]
        outbox[2 * tile, 0:8] = jnp.where(top_half, total, pltpu.roll(red, 4, 0))
        outbox[2 * tile, 8:16] = jnp.where(top_half, green, pltpu.roll(seen, 4, 0))
        outbox[2 * tile + 1, 0:8] = jnp.where(top_half, pltpu.roll(total, 4, 0), red)
        outbox[2 * tile + 1, 8:16] = jnp.where(top_half, pltpu.roll(green, 4, 0), seen)
        for target in (2 * tile, 2 * tile + 1):
            @pl.when(dep != target)
            def _():
                all_copy(target, dep).start()

            @pl.when(dep == target)
            def _():
                inbox[target] = outbox[target]

        return carry

    begun = 0
    for chunk in range(chunks):
        done = tiles if chunk == chunks - 1 else (chunk + 1) * (chunk_rows // 8) - 1
        finish_chunk(1, chunk)
        lax.fori_loop(begun, done, back_tile, 0)
        finish_chunk(0, chunk)
        lax.fori_loop(begun, done, outer_tile, 0)
        begun = done

    def compose(source, state):
        seen, upper, lower = state

        @pl.when(source != dep)
        def _():
            all_copy(source, source).wait_recv()

        first, second = inbox[source, 0:8, :], inbox[source, 8:16, :]
        through = jnp.where(top_half, pltpu.roll(second, 4, 0), second)
        return seen * through, upper + seen * first, lower + seen * second

    seen, upper, lower = lax.fori_loop(0, depth_count, compose, (ones, zeros, zeros))
    total, red = upper[0:4], upper[4:8]
    out_ref[0] = -0.5 * (total + red)
    out_ref[1] = -lower[0:4]
    out_ref[2] = -0.5 * (total - red)
    out_ref[3] = seen[0:4] - 1.0

    for group in range(groups):
        for side, exists in ((0, has_prev), (1, has_next)):
            @pl.when(exists)
            def _():
                img_copy(side, group).wait_send()

    for side, exists in ((0, has_front), (1, has_back)):
        @pl.when(exists)
        def _():
            edge_copy(side).wait_send()
            for chunk in range(chunks):
                depth_copy(side, chunk).wait_send()

    def finish(target, carry):
        @pl.when(target != dep)
        def _():
            all_copy(target, target).wait_send()

        return carry

    lax.fori_loop(0, depth_count, finish, 0)

    for chunk in range(relays):
        for side in range(2):
            @pl.when(passes_on(side, chunk))
            def _():
                pass_copy(side, chunk).wait_send()

    for side, relaying in img_relays:
        @pl.when(relaying)
        def _():
            for group in round_groups:
                pass_img_copy(side, group).wait_send()


def solution(mesh):
    img_count, depth_count = mesh.shape["img"], mesh.shape["depth"]

    def local(counts):
        slab, rows, columns = counts.shape
        ext = rows + 16
        groups = slab // 8

        def body(*refs):
            render_kernel(slab * depth_count, img_count, depth_count, *refs)

        anywhere = pl.BlockSpec(memory_space=pl.ANY)
        layers = pl.pallas_call(
            body,
            out_shape=jax.ShapeDtypeStruct((4, rows // depth_count, columns), f32),
            in_specs=[anywhere] * 3,
            out_specs=pl.BlockSpec(memory_space=pltpu.VMEM),
            scratch_shapes=[
                pltpu.VMEM((slab, rows, columns), jnp.int32),
                pltpu.VMEM((2, columns, columns), bf16),
                pltpu.VMEM((ext, 3 * ext + 16), f32),
                pltpu.VMEM((ext, 3 * ext + 16), bf16),
                pltpu.VMEM((2, groups, 5, 8, columns), jnp.int32),
                pltpu.VMEM((2, groups, 5, 8, columns), jnp.int32),
                pltpu.VMEM((8, 16, columns), f32),
                pltpu.VMEM((slab, ext, columns), bf16),
                pltpu.VMEM((slab, ext + 16, columns), bf16),
                pltpu.VMEM((slab + 10, ext, columns), f32),
                pltpu.VMEM((slab + 2, ext, columns), f32),
                pltpu.VMEM((2, 8, columns), f32),
                pltpu.VMEM((2, 8, columns), f32),
                pltpu.VMEM((4, rows // 8, 8, columns), f32),
                pltpu.VMEM((depth_count, 16, columns), f32),
                pltpu.VMEM((depth_count, 16, columns), f32),
                pltpu.VMEM((depth_count // run, 5, rows * run // depth_count, columns), f32),
                pltpu.SemaphoreType.DMA((5,)),
                pltpu.SemaphoreType.DMA((2, groups)),
                pltpu.SemaphoreType.DMA((2, groups)),
                pltpu.SemaphoreType.DMA((2, depth_count // run + 1)),
                pltpu.SemaphoreType.DMA((2, depth_count // run + 1)),
                pltpu.SemaphoreType.DMA((depth_count,)),
                pltpu.SemaphoreType.DMA((depth_count,)),
                pltpu.SemaphoreType.DMA((depth_count // run,)),
                pltpu.SemaphoreType.DMA((depth_count // run,)),
                pltpu.VMEM((2, 5, 8, columns), jnp.int32),
                pltpu.SemaphoreType.DMA((2,)),
                pltpu.SemaphoreType.DMA((2,)),
            ],
            compiler_params=pltpu.CompilerParams(
                collective_id=0, has_side_effects=True, vmem_limit_bytes=56 << 20
            ),
        )(counts, jnp.asarray(column_matrix(columns)), jnp.asarray(row_matrix(rows)))
        return -layers

    return jax.shard_map(
        local,
        mesh=mesh,
        in_specs=(P("depth", "img", None),),
        out_specs=P(None, ("img", "depth"), None),
        check_vma=False,
    )
```

```python
import math

import jax
import jax.numpy as jnp
import numpy as np
from jax import lax
from jax.experimental import pallas as pl
from jax.experimental.pallas import tpu as pltpu
from jax.sharding import PartitionSpec as P
import ml_dtypes

gauss_taps = [
    math.exp(-offset * offset / 8.0)
    / sum((math.exp(-other * other / 8.0) for other in range(-4, 5)))
    for offset in range(-4, 5)
]
MESH = pl.DeviceIdType.MESH
f32 = jnp.float32
bf16 = jnp.bfloat16
run = 4
img_run = 4


def split_taps(matrix):
    high = matrix.astype(np.float32).astype(ml_dtypes.bfloat16).astype(np.float64)
    low = (matrix - high).astype(np.float32).astype(ml_dtypes.bfloat16).astype(np.float64)
    return high, low


def column_matrix(columns):
    index = np.arange(columns)
    offset = index[:, None] - index[None, :]
    matrix = np.zeros((columns, columns))
    for k in range(-4, 5):
        matrix[offset == k] = gauss_taps[k + 4]
    high, low = split_taps(matrix)
    return np.stack([high, low]).astype(ml_dtypes.bfloat16)


def row_matrix(rows):
    target = np.full((rows + 16,), 10**6)
    target[7 : rows + 9] = np.arange(-1, rows + 1)
    source = np.full((rows + 16,), -(10**6))
    source[:rows] = np.arange(rows)
    source[rows : rows + 5] = np.arange(-5, 0)
    source[rows + 8 : rows + 13] = np.arange(rows, rows + 5)
    offset = source[None, :] - target[:, None]
    matrix = np.zeros(offset.shape)
    for k in range(-4, 5):
        matrix[offset == k] = gauss_taps[k + 4]
    high, low = split_taps(matrix)
    pad = np.zeros((rows + 16, 16))
    return np.concatenate([high, low, high, pad], axis=1).astype(np.float32)


def render_kernel(
    depth_total, img_count, depth_count,
    counts_ref, colmat_ref, rowmat_ref, out_ref,
    cnt, wcol, brow_f, brow, stage, halo, hconv, yhigh, ylow, ufield, sfield,
    pack, pack_in, partial, outbox, inbox,
    relay, load_sem, img_send, img_recv, dep_send, dep_recv, all_send, all_recv,
    relay_send, relay_recv, img_relay, img_relay_send, img_relay_recv,
):
    img = lax.axis_index("img")
    dep = lax.axis_index("depth")
    slab, rows, columns = cnt.shape
    tiles = rows // 8
    owned = rows // depth_count
    ext = rows + 16
    chunks = dep_send.shape[1] - 1
    chunk_rows = rows // chunks

    barrier = pltpu.get_barrier_semaphore()
    has_prev, has_next = img > 0, img < img_count - 1
    has_front, has_back = dep > 0, dep < depth_count - 1

    def greet_depth(step, carry):
        target = lax.rem(dep + step, depth_count)
        pl.semaphore_signal(barrier, inc=1, device_id=(img, target), device_id_type=MESH)
        return carry

    lax.fori_loop(1, depth_count, greet_depth, 0)
    img_partners = [
        step for near in (1, img_run - 1, img_run) for step in (near, img_count - near)
    ]
    for step in img_partners:
        pl.semaphore_signal(
            barrier, inc=1, device_id=(lax.rem(img + step, img_count), dep), device_id_type=MESH
        )

    def load_rows(start, size, sem):
        span = pl.ds(start, size)
        return pltpu.make_async_copy(counts_ref.at[:, span, :], cnt.at[:, span, :], sem)

    loads = [
        load_rows(0, 8, load_sem.at[0]),
        load_rows(rows - 8, 8, load_sem.at[1]),
        load_rows(8, rows - 16, load_sem.at[2]),
        pltpu.make_async_copy(colmat_ref, wcol, load_sem.at[3]),
        pltpu.make_async_copy(rowmat_ref, brow_f, load_sem.at[4]),
    ]
    for load in loads:
        load.start()

    ylow[:, ext:, :] = jnp.zeros((slab, 16, columns), bf16)
    hconv[...] = jnp.zeros(hconv.shape, f32)

    @pl.when(jnp.logical_not(has_prev))
    def _():
        halo[0] = jnp.zeros(halo.shape[1:], jnp.int32)

    @pl.when(jnp.logical_not(has_next))
    def _():
        halo[1] = jnp.zeros(halo.shape[1:], jnp.int32)

    @pl.when(jnp.logical_not(has_front))
    def _():
        ufield[0:5] = jnp.zeros((5, ext, columns), f32)
        pack_in[0] = jnp.zeros(pack_in.shape[1:], f32)

    @pl.when(jnp.logical_not(has_back))
    def _():
        ufield[slab + 5 :] = jnp.zeros((5, ext, columns), f32)
        pack_in[1] = jnp.zeros(pack_in.shape[1:], f32)

    for load in loads[:2]:
        load.wait()

    for group in range(slab // 8):
        for r in range(5):
            stage[0, group, r] = cnt[group * 8 : group * 8 + 8, r, :]
            stage[1, group, r] = cnt[group * 8 : group * 8 + 8, rows - 5 + r, :]

    pl.semaphore_wait(barrier, depth_count - 1 + len(img_partners))

    def img_copy(side, group):
        target = lax.rem(img + (img_count - 1 if side == 0 else 1), img_count)
        return pltpu.make_async_remote_copy(
            src_ref=stage.at[side, group],
            dst_ref=halo.at[1 - side, group],
            send_sem=img_send.at[side, group],
            recv_sem=img_recv.at[1 - side, group],
            device_id=(target, dep),
            device_id_type=MESH,
        )

    def goes_round_img(side, group):
        if group not in round_groups:
            return False
        return img == (img_run if side == 0 else img_count - 1 - img_run)

    def round_img_copy(side, group):
        return pltpu.make_async_remote_copy(
            src_ref=stage.at[side, group],
            dst_ref=img_relay.at[group - round_groups[0]],
            send_sem=img_send.at[side, group],
            recv_sem=img_relay_recv.at[group - round_groups[0]],
            device_id=(lax.rem(img + (img_count - img_run if side == 0 else img_run), img_count), dep),
            device_id_type=MESH,
        )

    def pass_img_copy(side, group):
        step = img_run - 1 if side == 0 else img_count - img_run + 1
        return pltpu.make_async_remote_copy(
            src_ref=img_relay.at[group - round_groups[0]],
            dst_ref=halo.at[1 - side, group],
            send_sem=img_relay_send.at[group - round_groups[0]],
            recv_sem=img_recv.at[1 - side, group],
            device_id=(lax.rem(img + step, img_count), dep),
            device_id_type=MESH,
        )

    groups = slab // 8
    round_groups = (2,)
    img_relays = ((0, img == 0), (1, img == img_count - 1))
    order = [0, groups - 1] + list(range(1, groups - 1))
    for side in range(2):
        for group in round_groups:
            @pl.when(goes_round_img(side, group))
            def _():
                round_img_copy(side, group).start()

    for group in order:
        for side, exists in ((0, has_prev), (1, has_next)):
            round_trip = goes_round_img(side, group)

            @pl.when(exists & jnp.logical_not(round_trip))
            def _():
                img_copy(side, group).start()


    for load in loads[2:]:
        load.wait()

    row_id = lax.broadcasted_iota(jnp.int32, brow_f.shape, 0)
    outside = ((row_id == 7) & (img == 0)) | ((row_id == rows + 8) & (img == img_count - 1))
    brow[...] = jnp.where(outside, 0.0, brow_f[...]).astype(bf16)

    def column_smooth(block):
        block = block.astype(f32).astype(bf16)
        return jnp.dot(block, wcol[0], preferred_element_type=f32) + jnp.dot(
            block, wcol[1], preferred_element_type=f32
        )

    def halves(value):
        high = value.astype(bf16)
        return high, (value - high.astype(f32)).astype(bf16)

    def own_columns(step, carry):
        at = pl.ds(step * 4, 4)
        smooth = column_smooth(cnt[at].reshape(4 * rows, columns))
        high, low = halves(smooth)
        yhigh[at, :rows, :] = high.reshape(4, rows, columns)
        ylow[at, :rows, :] = low.reshape(4, rows, columns)
        return carry

    def pass_rows():
        for side, relaying in img_relays:
            @pl.when(relaying)
            def _():
                for group in round_groups:
                    round_img_copy(side, group).wait_recv()
                    pass_img_copy(side, group).start()

    def rows_of_group(group):
        lax.fori_loop(group * 2, group * 2 + 2, own_columns, 0)
        for side, exists in ((0, has_prev), (1, has_next)):
            @pl.when(exists)
            def _():
                img_copy(1 - side, group).wait_recv()

        for side in range(2):
            smooth = column_smooth(halo[side, group].reshape(40, columns))
            for r in range(5):
                hconv[:, side * 8 + r, :] = smooth[r * 8 : r * 8 + 8]

        def one_layer(j, carry):
            layer = group * 8 + j
            high, low = halves(hconv[j])
            yhigh[layer, rows:ext, :] = high
            ylow[layer, rows:ext, :] = low
            tall = yhigh[layer]
            field = jnp.concatenate([tall, tall, ylow[layer]], axis=0)
            ufield[layer + 5] = jnp.dot(brow[...], field, preferred_element_type=f32)
            return carry

        lax.fori_loop(0, 8, one_layer, 0)

    def depth_target(side):
        return lax.rem(dep + (depth_count - 1 if side == 0 else 1), depth_count)

    def depth_copy(side, chunk):
        source = 5 if side == 0 else slab
        place = slab + 5 if side == 0 else 0
        span = pl.ds(8 + chunk * chunk_rows, chunk_rows)
        return pltpu.make_async_remote_copy(
            src_ref=ufield.at[source : source + 5, span, :],
            dst_ref=ufield.at[place : place + 5, span, :],
            send_sem=dep_send.at[side, chunk],
            recv_sem=dep_recv.at[1 - side, chunk],
            device_id=(img, depth_target(side)),
            device_id_type=MESH,
        )

    stretch = lax.div(dep, run)
    relays = depth_count // run - 1

    def goes_round(side, chunk):
        if side == 0:
            return has_front & (lax.rem(dep, run) == 0) & (chunk < relays + 1 - stretch)
        return has_back & (lax.rem(dep, run) == run - 1) & (chunk <= stretch)

    def round_copy(side, chunk):
        source = 5 if side == 0 else slab
        step = depth_count - run if side == 0 else run
        return pltpu.make_async_remote_copy(
            src_ref=ufield.at[source : source + 5, pl.ds(8 + chunk * chunk_rows, chunk_rows), :],
            dst_ref=relay.at[chunk],
            send_sem=dep_send.at[side, chunk],
            recv_sem=relay_recv.at[chunk],
            device_id=(img, lax.rem(dep + step, depth_count)),
            device_id_type=MESH,
        )

    def passes_on(side, chunk):
        if side == 0:
            return (lax.rem(dep, run) == 0) & (chunk < relays - stretch)
        return (lax.rem(dep, run) == run - 1) & (chunk < stretch)

    def pass_copy(side, chunk):
        place = slab + 5 if side == 0 else 0
        step = run - 1 if side == 0 else depth_count - run + 1
        return pltpu.make_async_remote_copy(
            src_ref=relay.at[chunk],
            dst_ref=ufield.at[place : place + 5, pl.ds(8 + chunk * chunk_rows, chunk_rows), :],
            send_sem=relay_send.at[chunk],
            recv_sem=dep_recv.at[1 - side, chunk],
            device_id=(img, lax.rem(dep + step, depth_count)),
            device_id_type=MESH,
        )

    def pass_on(chunk):
        for side in range(2):
            @pl.when(passes_on(side, chunk))
            def _():
                round_copy(side, chunk).wait_recv()
                pass_copy(side, chunk).start()

    def edge_copy(side):
        return pltpu.make_async_remote_copy(
            src_ref=pack.at[side],
            dst_ref=pack_in.at[1 - side],
            send_sem=dep_send.at[side, chunks],
            recv_sem=dep_recv.at[1 - side, chunks],
            device_id=(img, depth_target(side)),
            device_id_type=MESH,
        )

    def pack_edges(side):
        first = 5 if side == 0 else slab + 1
        for j in range(4):
            pack[side, j : j + 1] = ufield[first + j, 7:8, :]
            pack[side, 4 + j : 5 + j] = ufield[first + j, rows + 8 : rows + 9, :]

    faces = ((0, has_front), (1, has_back))

    for side, group in ((0, 0), (1, groups - 1)):
        rows_of_group(group)
        if side == 0:
            pass_rows()
        pack_edges(side)

        @pl.when(faces[side][1])
        def _():
            edge_copy(side).start()

        for chunk in range(chunks):
            round_trip = goes_round(side, chunk)

            @pl.when(round_trip)
            def _():
                round_copy(side, chunk).start()

            @pl.when(faces[side][1] & jnp.logical_not(round_trip))
            def _():
                depth_copy(side, chunk).start()

    for group in range(1, groups - 1):
        rows_of_group(group)

    def depth_smooth(low, high, first, last):
        def one_tile(tile, carry):
            r = pl.ds(pl.multiple_of(lax.div(tile, columns // 128) * 8, 8), 8)
            c = pl.ds(pl.multiple_of(lax.rem(tile, columns // 128) * 128, 128), 128)
            held = [ufield[m, r, c] for m in range(low, low + 8)]
            for m in range(low, high):
                held.append(ufield[m + 8, r, c])
                total = gauss_taps[4] * held[4]
                for k in range(4):
                    total = total + gauss_taps[k] * (held[k] + held[8 - k])
                sfield[m, r, c] = total
                held.pop(0)
            return carry

        per_row = columns // 128
        lax.fori_loop(first * per_row, last * per_row, one_tile, 0)

    column_id = lax.broadcasted_iota(jnp.int32, (8, columns), 1)
    at_left, at_right = column_id == 0, column_id == columns - 1
    row_in_tile = lax.broadcasted_iota(jnp.int32, (8, columns), 0)
    is_first_row, is_last_row = row_in_tile == 0, row_in_tile == 7

    def shade_layer(layer, tile, state):
        seen, total, red, green = state
        base = pl.multiple_of(8 + 8 * tile, 8)
        span = pl.ds(base, 8)
        here = sfield[layer + 1, span, :]
        dz = sfield[layer + 2, span, :] - sfield[layer, span, :]
        above = sfield[layer + 1, pl.ds(pl.multiple_of(8 * tile, 8), 8), :]
        below = sfield[layer + 1, pl.ds(pl.multiple_of(16 + 8 * tile, 8), 8), :]
        before = pltpu.roll(jnp.where(is_last_row, above, here), 1, 0)
        after = pltpu.roll(jnp.where(is_first_row, below, here), 7, 0)
        dx = after - before
        left = jnp.where(at_left, 0.0, pltpu.roll(here, 1, 1))
        right = jnp.where(at_right, 0.0, pltpu.roll(here, columns - 1, 1))
        dy = right - left
        shading = 0.55 + 0.45 * jnp.tanh(0.72 * dz + 0.9 * dx + 0.96 * dy)
        square = here * here
        bend = dz * dz + dx * dx + dy * dy
        tau = (square * pl.reciprocal(1.0 + square)) * ((1.0 + bend) * (1.5 / depth_total))
        weight = seen * (1.0 - jnp.exp(-tau))
        light = weight * shading
        centred = here - 2.5
        return (
            seen - weight,
            total + light,
            red + light * jnp.tanh(centred),
            green + light * jnp.exp(-(centred * centred)),
        )

    pass_on(0)
    depth_smooth(5, slab - 3, 0, ext // 8)
    zeros = jnp.zeros((8, columns), f32)
    ones = jnp.ones((8, columns), f32)
    def shade_layers(first, last, tile, state):
        return lax.fori_loop(
            first,
            last,
            lambda layer, state: shade_layer(layer, tile, state),
            state,
            unroll=min(last - first, 11),
        )

    def inner_tile(tile, carry):
        state = shade_layers(5, slab - 5, tile, (ones, zeros, zeros, zeros))
        for part in range(4):
            partial[part, tile] = state[part]
        return carry

    pass_on(1)
    lax.fori_loop(0, 3, inner_tile, 0)
    pass_on(2)
    lax.fori_loop(3, tiles, inner_tile, 0)

    for side, exists in faces:
        @pl.when(exists)
        def _():
            edge_copy(1 - side).wait_recv()

    for j in range(4):
        ufield[1 + j, 7:8, :] = pack_in[0, j : j + 1]
        ufield[1 + j, rows + 8 : rows + 9, :] = pack_in[0, 4 + j : 5 + j]
        ufield[slab + 5 + j, 7:8, :] = pack_in[1, j : j + 1]
        ufield[slab + 5 + j, rows + 8 : rows + 9, :] = pack_in[1, 4 + j : 5 + j]

    def finish_chunk(side, chunk):
        @pl.when(faces[side][1])
        def _():
            depth_copy(1 - side, chunk).wait_recv()

        tiles_per = chunk_rows // 8
        first = 1 + chunk * tiles_per if chunk > 0 else 0
        last = 1 + (chunk + 1) * tiles_per if chunk < chunks - 1 else ext // 8
        span = slice(first * 8, last * 8)
        if side == 0:
            depth_smooth(0, 5, first, last)
        else:
            depth_smooth(slab - 3, slab + 2, first, last)

        @pl.when(jnp.logical_not(faces[side][1]))
        def _():
            beyond = 0 if side == 0 else slab + 1
            sfield[beyond, span, :] = jnp.zeros((last * 8 - first * 8, columns), f32)

    def all_copy(target, source):
        return pltpu.make_async_remote_copy(
            src_ref=outbox.at[target],
            dst_ref=inbox.at[source],
            send_sem=all_send.at[target],
            recv_sem=all_recv.at[source],
            device_id=(img, target),
            device_id_type=MESH,
        )

    top_half = row_in_tile < 4
    def back_tile(tile, carry):
        state = shade_layers(slab - 5, slab, tile, (ones, zeros, zeros, zeros))
        seen = partial[0, tile]
        for part in range(1, 4):
            partial[part, tile] = partial[part, tile] + seen * state[part]
        partial[0, tile] = seen * state[0]
        return carry

    def outer_tile(tile, carry):
        state = shade_layers(0, 5, tile, (ones, zeros, zeros, zeros))
        total, red, green = (
            state[part] + state[0] * partial[part, tile] for part in range(1, 4)
        )
        seen = state[0] * partial[0, tile]
        outbox[2 * tile, 0:8] = jnp.where(top_half, total, pltpu.roll(red, 4, 0))
        outbox[2 * tile, 8:16] = jnp.where(top_half, green, pltpu.roll(seen, 4, 0))
        outbox[2 * tile + 1, 0:8] = jnp.where(top_half, pltpu.roll(total, 4, 0), red)
        outbox[2 * tile + 1, 8:16] = jnp.where(top_half, pltpu.roll(green, 4, 0), seen)
        for target in (2 * tile, 2 * tile + 1):
            @pl.when(dep != target)
            def _():
                all_copy(target, dep).start()

            @pl.when(dep == target)
            def _():
                inbox[target] = outbox[target]

        return carry

    begun = 0
    for chunk in range(chunks):
        done = tiles if chunk == chunks - 1 else (chunk + 1) * (chunk_rows // 8) - 1
        finish_chunk(1, chunk)
        lax.fori_loop(begun, done, back_tile, 0)
        finish_chunk(0, chunk)
        lax.fori_loop(begun, done, outer_tile, 0)
        begun = done

    def compose(source, state):
        seen, upper, lower = state

        @pl.when(source != dep)
        def _():
            all_copy(source, source).wait_recv()

        first, second = inbox[source, 0:8, :], inbox[source, 8:16, :]
        through = jnp.where(top_half, pltpu.roll(second, 4, 0), second)
        return seen * through, upper + seen * first, lower + seen * second

    seen, upper, lower = lax.fori_loop(0, depth_count, compose, (ones, zeros, zeros))
    total, red = upper[0:4], upper[4:8]
    out_ref[0] = -0.5 * (total + red)
    out_ref[1] = -lower[0:4]
    out_ref[2] = -0.5 * (total - red)
    out_ref[3] = seen[0:4] - 1.0

    for group in range(groups):
        for side, exists in ((0, has_prev), (1, has_next)):
            @pl.when(exists)
            def _():
                img_copy(side, group).wait_send()

    for side, exists in ((0, has_front), (1, has_back)):
        @pl.when(exists)
        def _():
            edge_copy(side).wait_send()
            for chunk in range(chunks):
                depth_copy(side, chunk).wait_send()

    def finish(target, carry):
        @pl.when(target != dep)
        def _():
            all_copy(target, target).wait_send()

        return carry

    lax.fori_loop(0, depth_count, finish, 0)

    for chunk in range(relays):
        for side in range(2):
            @pl.when(passes_on(side, chunk))
            def _():
                pass_copy(side, chunk).wait_send()

    for side, relaying in img_relays:
        @pl.when(relaying)
        def _():
            for group in round_groups:
                pass_img_copy(side, group).wait_send()


def solution(mesh):
    img_count, depth_count = mesh.shape["img"], mesh.shape["depth"]

    def local(counts):
        slab, rows, columns = counts.shape
        ext = rows + 16
        groups = slab // 8

        def body(*refs):
            render_kernel(slab * depth_count, img_count, depth_count, *refs)

        anywhere = pl.BlockSpec(memory_space=pl.ANY)
        layers = pl.pallas_call(
            body,
            out_shape=jax.ShapeDtypeStruct((4, rows // depth_count, columns), f32),
            in_specs=[anywhere] * 3,
            out_specs=pl.BlockSpec(memory_space=pltpu.VMEM),
            scratch_shapes=[
                pltpu.VMEM((slab, rows, columns), jnp.int32),
                pltpu.VMEM((2, columns, columns), bf16),
                pltpu.VMEM((ext, 3 * ext + 16), f32),
                pltpu.VMEM((ext, 3 * ext + 16), bf16),
                pltpu.VMEM((2, groups, 5, 8, columns), jnp.int32),
                pltpu.VMEM((2, groups, 5, 8, columns), jnp.int32),
                pltpu.VMEM((8, 16, columns), f32),
                pltpu.VMEM((slab, ext, columns), bf16),
                pltpu.VMEM((slab, ext + 16, columns), bf16),
                pltpu.VMEM((slab + 10, ext, columns), f32),
                pltpu.VMEM((slab + 2, ext, columns), f32),
                pltpu.VMEM((2, 8, columns), f32),
                pltpu.VMEM((2, 8, columns), f32),
                pltpu.VMEM((4, rows // 8, 8, columns), f32),
                pltpu.VMEM((depth_count, 16, columns), f32),
                pltpu.VMEM((depth_count, 16, columns), f32),
                pltpu.VMEM((depth_count // run, 5, rows * run // depth_count, columns), f32),
                pltpu.SemaphoreType.DMA((5,)),
                pltpu.SemaphoreType.DMA((2, groups)),
                pltpu.SemaphoreType.DMA((2, groups)),
                pltpu.SemaphoreType.DMA((2, depth_count // run + 1)),
                pltpu.SemaphoreType.DMA((2, depth_count // run + 1)),
                pltpu.SemaphoreType.DMA((depth_count,)),
                pltpu.SemaphoreType.DMA((depth_count,)),
                pltpu.SemaphoreType.DMA((depth_count // run,)),
                pltpu.SemaphoreType.DMA((depth_count // run,)),
                pltpu.VMEM((2, 5, 8, columns), jnp.int32),
                pltpu.SemaphoreType.DMA((2,)),
                pltpu.SemaphoreType.DMA((2,)),
            ],
            compiler_params=pltpu.CompilerParams(
                collective_id=0, has_side_effects=True, vmem_limit_bytes=56 << 20
            ),
        )(counts, jnp.asarray(column_matrix(columns)), jnp.asarray(row_matrix(rows)))
        return -layers

    return jax.shard_map(
        local,
        mesh=mesh,
        in_specs=(P("depth", "img", None),),
        out_specs=P(None, ("img", "depth"), None),
        check_vma=False,
    )
```
